128 devices in a mesh: row: 64 (over z, y, x), col: 2 (over core).
Axes of the slice: x: 4, y: 4, z: 4, core: 2. Of those that a mesh axis runs over, the one named last changes fastest.
Arguments:
- gate_weight: bfloat16 [8192, 29568], P('row', 'col'), may hold values from -800 to 800
- up_weight: bfloat16 [8192, 29568], P('row', 'col'), may hold values from -800 to 800
- down_weight: bfloat16 [29568, 8192], P('row', 'col'), may hold values from -800 to 800
- gate_in: bfloat16 [8192, 64], P(('row', 'col')), may hold values from -6 to 6
- gate_out: bfloat16 [64, 29568], P(None, 'col'), may hold values from -3 to 3
- up_in: bfloat16 [8192, 64], P(('row', 'col')), may hold values from -6 to 6
- up_out: bfloat16 [64, 29568], P(None, 'col'), may hold values from -3 to 3
- down_in: bfloat16 [29568, 64], P(('row', 'col')), may hold values from -6 to 6
- down_out: bfloat16 [64, 8192], P(None, 'col'), may hold values from -3 to 3
- gate_magnitude: float32 [29568], P('col'), may hold values from 20 to 400
- up_magnitude: float32 [29568], P('col'), may hold values from 20 to 400
- down_magnitude: float32 [8192], P('col'), may hold values from 20 to 400
Outputs:
- gate_merged: bfloat16 [8192, 29568], P(None, ('col', 'row'))
- up_merged: bfloat16 [8192, 29568], P(None, ('col', 'row'))
- down_merged: bfloat16 [29568, 8192], P(None, ('col', 'row'))
The draws below stay inside these ranges and needn't reach their ends.
All inputs are finite; a program needn't handle non-finite values.
Results may differ from the reference program's by a relative error of at most 0.0029.
Values may be sent and summed in bfloat16 or wider, within the bound.
A program may use at most 192 MiB of HBM per device.

```python
import math
import jax
import jax.numpy as jnp
from jax import lax

D = 8192
FF = 29568
RANK = 64


def draw_matrix(key, height, breadth):
    first, second, third = jax.random.split(key, 3)
    rising = 3.0 ** (jnp.arange(height, dtype=jnp.float32) / height)
    base = jnp.clip(jax.random.normal(first, (height, breadth), jnp.float32), -4.0, 4.0)
    row_scale = jnp.exp(jax.random.uniform(second, (height,), jnp.float32, 0.0, math.log(10.0)))
    col_scale = jnp.exp(jax.random.uniform(third, (breadth,), jnp.float32, 0.0, math.log(10.0)))
    values = 0.4 * base * (row_scale * rising)[:, None] * col_scale[None, :]
    return values.astype(jnp.bfloat16)


def draw_gate_weight(key, part):
    return draw_matrix(jax.random.fold_in(key, 11), D, FF)


def draw_up_weight(key, part):
    return draw_matrix(jax.random.fold_in(key, 23), D, FF)


def draw_down_weight(key, part):
    return draw_matrix(jax.random.fold_in(key, 37), FF, D)


def shard_levels(stream_key, dims, cuts, smallest, top_value):
    gain, own = 1.0, jax.random.fold_in(stream_key, 6)
    for dim, shards_of in cuts:
        heights = jnp.exp(jax.random.uniform(jax.random.fold_in(own, dim), (shards_of,), jnp.float32, smallest / len(cuts), top_value / len(cuts)))
        gain = gain * jnp.repeat(heights, dims[dim] // shards_of).reshape([-1 if axis == dim else 1 for axis in range(len(dims))])
    return gain


def normal_values(key, shape, scale, limit, shards=(), kind=jnp.bfloat16):
    result = scale * jax.random.normal(key, shape, jnp.float32)
    if shards:
        result = result * shard_levels(key, shape, shards, -0.22, 0.18)
    return jnp.clip(result, -limit, limit).astype(kind)


def setup_inputs(seed: int = 0) -> dict:
    seeds = jax.random.split(jax.random.key(seed), 13)
    gate_weight = draw_gate_weight(jax.random.fold_in(seeds[12], 71), 0)
    up_weight = draw_up_weight(jax.random.fold_in(seeds[12], 71), 0)
    down_weight = draw_down_weight(jax.random.fold_in(seeds[12], 71), 0)
    gate_in = normal_values(seeds[3], (D, RANK), 1.0, 6.0, ((0, 128),))
    gate_out = normal_values(seeds[4], (RANK, FF), 0.5, 3.0, ((1, 2),))
    up_in = normal_values(seeds[5], (D, RANK), 1.0, 6.0, ((0, 128),))
    up_out = normal_values(seeds[6], (RANK, FF), 0.5, 3.0, ((1, 2),))
    down_in = normal_values(seeds[7], (FF, RANK), 1.0, 6.0, ((0, 128),))
    down_out = normal_values(seeds[8], (RANK, D), 0.5, 3.0, ((1, 2),))
    gate_magnitude = jnp.clip(jnp.exp(math.log(400.0) - 2.9957323 * jax.random.uniform(seeds[9], (FF,), jnp.float32) ** shard_levels(seeds[9], (FF,), ((0, 2),), -0.2, 0.2)), 20.0, 400.0)
    up_magnitude = jnp.clip(jnp.exp(math.log(400.0) - 2.9957323 * jax.random.uniform(seeds[10], (FF,), jnp.float32) ** shard_levels(seeds[10], (FF,), ((0, 2),), -0.2, 0.2)), 20.0, 400.0)
    down_magnitude = jnp.clip(jnp.exp(math.log(400.0) - 2.9957323 * jax.random.uniform(seeds[11], (D,), jnp.float32) ** shard_levels(seeds[11], (D,), ((0, 2),), -0.2, 0.2)), 20.0, 400.0)
    return {"gate_weight": gate_weight, "up_weight": up_weight, "down_weight": down_weight, "gate_in": gate_in, "gate_out": gate_out, "up_in": up_in, "up_out": up_out, "down_in": down_in, "down_out": down_out, "gate_magnitude": gate_magnitude, "up_magnitude": up_magnitude, "down_magnitude": down_magnitude}


epsilon = 1e-06

def merge_matrix(weight, factor_rows, factor_cols, magnitude):
    update = jnp.dot(factor_rows, factor_cols, preferred_element_type=jnp.float32)
    combined = weight.astype(jnp.float32) + update
    squares = lax.optimization_barrier(jnp.sum(combined * combined, axis=0))
    column_scale = magnitude / jnp.sqrt(squares + epsilon)
    return (combined * column_scale[None, :]).astype(jnp.bfloat16)

def reference(gate_weight, up_weight, down_weight, gate_in, gate_out, up_in, up_out, down_in, down_out, gate_magnitude, up_magnitude, down_magnitude):
    gate_merged = merge_matrix(gate_weight, gate_in, gate_out, gate_magnitude)
    up_merged = merge_matrix(up_weight, up_in, up_out, up_magnitude)
    down_merged = merge_matrix(down_weight, down_in, down_out, down_magnitude)
    return (gate_merged, up_merged, down_merged)
```

```python
import functools

import jax
import jax.numpy as jnp
from jax import lax
from jax.experimental import pallas as pl
from jax.experimental.pallas import tpu as pltpu
from jax.sharding import PartitionSpec as P

MESH = pl.DeviceIdType.MESH
BF = jnp.bfloat16
F32 = jnp.float32
EPS = 1e-06
RANK = 64
N = 64
COLS = 14784
SLAB = 231
DROWS = 462
DCOLS = 4096
WINDOW = 512
BLK = 1024
ORDERS = ((2, 1, 0), (1, 0, 2), (0, 2, 1))
FIRST = (0, 120, 240)
PARTS = ((0, 96), (96, 88), (184, 88))
CHUNKS = (((0, 128), (128, 104)), ((0, 128), (128, 104)), ((0, 32), (32, 32)))


def peer_of(me, axis, k):
    stride = (16, 4, 1)[axis]
    mine = lax.rem(lax.div(me, stride), 4)
    other = lax.rem(mine + k, 4)
    return me + (other - mine) * stride, mine, other


def greet(me, core, partner):
    bar = pltpu.get_barrier_semaphore()
    for axis in range(3):
        for k in (1, 2, 3):
            p, _, _ = peer_of(me, axis, k)
            pl.semaphore_signal(bar, inc=1, device_id=(p, core), device_id_type=MESH)
    if partner:
        pl.semaphore_signal(bar, inc=1, device_id=(me, 1 - core), device_id_type=MESH)
    pl.semaphore_wait(bar, 10 if partner else 9)


def eye(h):
    return lax.broadcasted_iota(jnp.int32, (h, 128), 0) == lax.broadcasted_iota(
        jnp.int32, (h, 128), 1
    )


def to_lanes(x):
    n = x.shape[0]
    sums = jnp.sum(x, axis=1, keepdims=True)
    rows = []
    for b in range(0, n, 128):
        h = min(128, n - b)
        rows.append(jnp.sum(jnp.where(eye(h), sums[b : b + h], 0.0), axis=0, keepdims=True))
    return jnp.concatenate(rows, axis=0)


def to_sublanes(row, h):
    return jnp.sum(jnp.where(eye(h), row, 0.0), axis=1, keepdims=True)


def combined_t(w, q, p, start, n):
    upd = lax.dot_general(
        q[:, pl.ds(start, n)], p, (((0,), (1,)), ((), ())), preferred_element_type=F32
    )
    return w[pl.ds(start, n), :].astype(F32) + upd


def prep_kernel(
    wg, wu, wd, qg, qu, qd, pg, pu, pd, mags,
    og, ou, od,
    vg, vu, vd, sg, su, sd, full, turn, both_g, both_u, both_d, pdown, sums, got, scale,
    in_sem, p_send, p_recv, p_loc, r_send, r_recv, out_sem,
):
    me = lax.axis_index("row")
    core = lax.axis_index("col")
    loads = []
    for i, (src, dst) in enumerate(((wg, vg), (wu, vu), (wd, vd))):
        cp = pltpu.make_async_copy(src, dst, in_sem.at[i])
        cp.start()
        loads.append(cp)
    greet(me, core, True)
    ps = []
    for i, (src, dst) in enumerate(((pg, both_g), (pu, both_u), (pd, both_d))):
        far = pltpu.make_async_remote_copy(
            src_ref=src, dst_ref=dst.at[core], send_sem=p_send.at[i], recv_sem=p_recv.at[i],
            device_id=(me, 1 - core), device_id_type=MESH,
        )
        near = pltpu.make_async_copy(src, dst.at[core], p_loc.at[i])
        far.start()
        near.start()
        ps.append((far, near))
    for far, near in ps:
        near.wait()
        far.wait()

    for i, (w, q, both) in enumerate(((vg, qg, both_g), (vu, qu, both_u))):
        loads[i].wait()
        p = both[...].reshape(2 * RANK, RANK)

        def squares(b, carry, w=w, q=q, p=p, first=FIRST[i]):
            x = combined_t(w, q, p, pl.multiple_of(b * BLK, BLK), BLK)
            sums[0, pl.ds(pl.multiple_of(first + b * 8, 8), 8), :] = to_lanes(x * x)
            return carry

        lax.fori_loop(0, COLS // BLK, squares, 0)
        x = combined_t(w, q, p, COLS // BLK * BLK, COLS % BLK)
        sums[0, FIRST[i] + 112 : FIRST[i] + 116, :] = to_lanes(x * x)
        sums[0, FIRST[i] + 116 : FIRST[i] + 120, :] = jnp.zeros((4, 128), F32)
    pdown[0:231, :] = both_d[0].astype(F32).T
    pdown[231:462, :] = both_d[1].astype(F32).T
    p = pdown[0:DROWS, :].astype(BF)
    loads[2].wait()

    def down_block(j):
        at = pl.ds(pl.multiple_of(j * 128, 128), 128)
        upd = jnp.dot(p, qd[:, at], preferred_element_type=F32)
        return vd[:, at].astype(F32) + upd

    def squares_down(j, carry):
        x = down_block(j)
        sums[0, pl.ds(FIRST[2] + j, 1), :] = jnp.sum(x * x, axis=0, keepdims=True)
        return carry

    lax.fori_loop(0, DCOLS // 128, squares_down, 0)

    def exchange(ph, t):
        res = []
        at = pl.ds(*PARTS[t])
        for k in (2, 1, 3):
            q, _, _ = peer_of(me, ORDERS[t][ph], k)
            res.append(
                pltpu.make_async_remote_copy(
                    src_ref=sums.at[ph, at], dst_ref=got.at[ph, k - 1, at],
                    send_sem=r_send.at[ph, t, k - 1], recv_sem=r_recv.at[ph, t, k - 1],
                    device_id=(q, core), device_id_type=MESH,
                )
            )
        return res

    for t in range(3):
        for cp in exchange(0, t):
            cp.start()
    for ph in range(3):
        for t in range(3):
            for cp in exchange(ph, t):
                cp.wait_recv()
            at = pl.ds(*PARTS[t])
            total = sums[ph, at, :] + got[ph, 0, at, :] + got[ph, 1, at, :] + got[ph, 2, at, :]
            if ph < 2:
                sums[ph + 1, at, :] = total
                for cp in exchange(ph + 1, t):
                    cp.start()
            else:
                scale[at, :] = mags[at, :] / jnp.sqrt(total + EPS)
    for ph in range(3):
        for t in range(3):
            for cp in exchange(ph, t):
                cp.wait_send()

    outs = []
    for i, (w, q, both, s, o) in enumerate(
        ((vg, qg, both_g, sg, og), (vu, qu, both_u, su, ou))
    ):
        p = both[...].reshape(2 * RANK, RANK)

        def merge(b, carry, w=w, q=q, p=p, first=FIRST[i]):
            start = pl.multiple_of(b * BLK, BLK)
            x = combined_t(w, q, p, start, BLK)
            f = scale[pl.ds(pl.multiple_of(first + b * 8, 8), 8), :]
            for e in range(8):
                full[pl.ds(pl.multiple_of(start + e * 128, 128), 128), :] = x[
                    e * 128 : (e + 1) * 128
                ] * to_sublanes(f[e : e + 1], 128)
            return carry

        lax.fori_loop(0, COLS // BLK, merge, 0)
        start = COLS // BLK * BLK
        x = combined_t(w, q, p, start, COLS % BLK)
        f = scale[FIRST[i] + 112 : FIRST[i] + 116, :]
        for e in range(4):
            h = 128 if e < 3 else 64
            full[start + e * 128 : start + e * 128 + h, :] = x[
                e * 128 : e * 128 + h
            ] * to_sublanes(f[e : e + 1], h)
        full[COLS : COLS + 8, :] = jnp.zeros((8, 128), F32)

        def cut(g, carry, s=s):
            base = pl.multiple_of(g * (8 * SLAB), 8)
            for e in range(8):
                s[g * 8 + e] = full[pl.ds(base + e * SLAB, SLAB + 1), :].astype(BF)
            return carry

        lax.fori_loop(0, N // 8, cut, 0)
        cp = pltpu.make_async_copy(s, o, out_sem.at[i])
        cp.start()
        outs.append(cp)

    p = pdown[0:DROWS, :].astype(BF)
    turn[...] = jnp.zeros_like(turn)
    first = WINDOW - lax.rem(me * DROWS, WINDOW)

    def merge_down(j, carry):
        y = down_block(j) * scale[pl.ds(FIRST[2] + j, 1), :]
        turn[0:DROWS, :] = y
        turn[WINDOW : WINDOW + DROWS, :] = y
        z = turn[pl.ds(first, WINDOW), :].T.astype(BF)
        sd[2 * j] = z[0:64]
        sd[2 * j + 1] = z[64:128]
        return carry

    lax.fori_loop(0, DCOLS // 128, merge_down, 0)
    cp = pltpu.make_async_copy(sd, od, out_sem.at[2])
    cp.start()
    outs.append(cp)
    for cp in outs:
        cp.wait()


def prep(wg, wu, wd, qg, qu, qd, pg, pu, pd, mags):
    hbm = pl.BlockSpec(memory_space=pl.ANY)
    vmem = pl.BlockSpec(memory_space=pltpu.VMEM)
    slab = (N, SLAB + 1, 128)
    dslab = (N, 64, WINDOW)
    dma = pltpu.SemaphoreType.DMA
    return pl.pallas_call(
        prep_kernel,
        out_shape=[jax.ShapeDtypeStruct(s, BF) for s in (slab, slab, dslab)],
        in_specs=[hbm] * 3 + [vmem] * 7,
        out_specs=[hbm] * 3,
        scratch_shapes=[
            pltpu.VMEM((COLS, 128), BF), pltpu.VMEM((COLS, 128), BF),
            pltpu.VMEM((DROWS, DCOLS), BF),
            pltpu.VMEM(slab, BF), pltpu.VMEM(slab, BF), pltpu.VMEM(dslab, BF),
            pltpu.VMEM((COLS + 8, 128), F32), pltpu.VMEM((2 * WINDOW, 128), F32),
            pltpu.VMEM((2, 64, 64), BF), pltpu.VMEM((2, 64, 64), BF), pltpu.VMEM((2, 64, 231), BF),
            pltpu.VMEM((464, 64), F32),
            pltpu.VMEM((3, 272, 128), F32), pltpu.VMEM((3, 3, 272, 128), F32),
            pltpu.VMEM((272, 128), F32),
            dma((3,)), dma((3,)), dma((3,)), dma((3,)), dma((3, 3, 3)), dma((3, 3, 3)), dma((3,)),
        ],
        compiler_params=pltpu.CompilerParams(
            collective_id=0, has_side_effects=True, vmem_limit_bytes=60 * 2**20
        ),
        name="prepare",
    )(wg, wu, wd, qg, qu, qd, pg, pu, pd, mags)


def at(ref, axis, idx, chunk):
    ix = [slice(None)] * 3
    ix[axis] = idx
    return ref.at[(*ix, pl.ds(*chunk))]


def exchange_kernel(*refs):
    ins, outs, s1, s2 = refs[0:3], refs[3:6], refs[6:9], refs[9:12]
    send, recv, near = refs[12:15]
    me = lax.axis_index("row")
    core = lax.axis_index("col")
    greet(me, core, False)
    stages = [(ins[m], s1[m], s2[m], outs[m]) for m in range(3)]

    def copies(ph, ch, m):
        axis = ORDERS[m][ph]
        src, dst = stages[m][ph], stages[m][ph + 1]
        chunk = CHUNKS[m][ch]
        res = []
        for k in (2, 1, 3):
            p, mine, other = peer_of(me, axis, k)
            res.append(
                pltpu.make_async_remote_copy(
                    src_ref=at(src, axis, other, chunk), dst_ref=at(dst, axis, mine, chunk),
                    send_sem=send.at[ph, ch, m, k - 1], recv_sem=recv.at[ph, ch, m, k - 1],
                    device_id=(p, core), device_id_type=MESH,
                )
            )
        loc = pltpu.make_async_copy(
            at(src, axis, mine, chunk), at(dst, axis, mine, chunk), near.at[ph, ch, m]
        )
        return res, loc

    def arrived(ph, ch, m):
        res, loc = copies(ph, ch, m)
        for cp in res:
            cp.wait_recv()
        loc.wait()

    for ph in range(3):
        for ch in range(2):
            for m in range(3):
                if ph > 0:
                    arrived(ph - 1, ch, m)
                res, loc = copies(ph, ch, m)
                for cp in res:
                    cp.start()
                loc.start()
    for ch in range(2):
        for m in range(3):
            arrived(2, ch, m)
    for ph in range(3):
        for ch in range(2):
            for m in range(3):
                for cp in copies(ph, ch, m)[0]:
                    cp.wait_send()


def exchange_all(g, u, d):
    arrays = [a.reshape(4, 4, 4, *a.shape[1:]) for a in (g, u, d)]
    hbm = pl.BlockSpec(memory_space=pl.ANY)
    dma = pltpu.SemaphoreType.DMA
    outs = pl.pallas_call(
        exchange_kernel,
        out_shape=[jax.ShapeDtypeStruct(a.shape, BF) for a in arrays],
        in_specs=[hbm] * 3,
        out_specs=[hbm] * 3,
        scratch_shapes=[pltpu.VMEM(a.shape, BF) for a in arrays] * 2
        + [dma((3, 2, 3, 3)), dma((3, 2, 3, 3)), dma((3, 2, 3))],
        compiler_params=pltpu.CompilerParams(
            collective_id=1, has_side_effects=True, vmem_limit_bytes=60 * 2**20
        ),
        name="exchange",
    )(*arrays)
    return [o.reshape(N, *o.shape[3:]) for o in outs]


def join_kernel(x, o):
    for e in range(8):
        o[:, e * 128 : (e + 1) * 128] = x[e, 0:SLAB, :]


def join(x):
    return pl.pallas_call(
        join_kernel,
        grid=(N // 8,),
        out_shape=jax.ShapeDtypeStruct((SLAB, N * 128), BF),
        in_specs=[pl.BlockSpec((8, SLAB + 1, 128), lambda i: (i, 0, 0))],
        out_specs=pl.BlockSpec((SLAB, 1024), lambda i: (0, i)),
        name="join",
    )(x)


TILES = 33


def join_down_kernel(x, o):
    g = pl.program_id(0)

    def tile(i, carry):
        t = g * TILES + i
        s = lax.div(t * 128, DROWS)
        nxt = jnp.minimum(s + 1, N - 1)
        lanes = pl.ds(pl.multiple_of(lax.rem(t, 4) * 128, 128), 128)
        lane = t * 128 + lax.broadcasted_iota(jnp.int32, (64, 128), 1)
        a = x[s, :, lanes]
        b = x[nxt, :, lanes]
        o[:, pl.ds(pl.multiple_of(i * 128, 128), 128)] = jnp.where(lane < (s + 1) * DROWS, a, b)
        return carry

    lax.fori_loop(0, TILES, tile, 0)


def join_down(x):
    return pl.pallas_call(
        join_down_kernel,
        grid=(7,),
        out_shape=jax.ShapeDtypeStruct((64, 29568), BF),
        in_specs=[pl.BlockSpec((N, 64, WINDOW), lambda i: (0, 0, 0))],
        out_specs=pl.BlockSpec((64, TILES * 128), lambda i: (0, i)),
        name="join_down",
    )(x)


def local(wg, wu, wd, pg, qg, pu, qu, pd, qd, mg, mu, md):
    pad = jnp.zeros((15360 - COLS,), F32)
    mags = jnp.concatenate((mg, pad, mu, pad, md)).reshape(272, 128)
    g, u, d = prep(wg.T, wu.T, wd, qg, qu, qd, pg, pu, pd.T, mags)
    g, u, d = exchange_all(g, u, d)
    return join(g).T, join(u).T, join_down(d).T


def solution(mesh):
    placed = (
        P("row", "col"),
        P("row", "col"),
        P("row", "col"),
        P(("row", "col"), None),
        P(None, "col"),
        P(("row", "col"), None),
        P(None, "col"),
        P(("row", "col"), None),
        P(None, "col"),
        P("col"),
        P("col"),
        P("col"),
    )
    return jax.shard_map(
        local,
        mesh=mesh,
        in_specs=placed,
        out_specs=(P(None, ("col", "row")), P(None, ("col", "row")), P(None, ("col", "row"))),
        check_vma=False,
    )
```

```python
import functools

import jax
import jax.numpy as jnp
from jax import lax
from jax.experimental import pallas as pl
from jax.experimental.pallas import tpu as pltpu
from jax.sharding import PartitionSpec as P

MESH = pl.DeviceIdType.MESH
BF = jnp.bfloat16
F32 = jnp.float32
EPS = 1e-06
RANK = 64
N = 64
COLS = 14784
SLAB = 231
DROWS = 462
DCOLS = 4096
WINDOW = 512
BLK = 1024
ORDERS = ((2, 1, 0), (1, 0, 2), (0, 2, 1))
FIRST = (0, 120, 240)
SUM_ROWS = (
    ((0, 40), (40, 40), (80, 40)),
    ((120, 40), (160, 40), (200, 40)),
    ((240, 8), (248, 8), (256, 16)),
)
GROUPS = (
    (0, ((0, 80), (80, 80), (160, 72))),
    (1, ((0, 80), (80, 80), (160, 72))),
    (2, ((0, 48), (80, 48), (176, 48))),
    (2, ((48, 32), (128, 48), (224, 32))),
)


def peer_of(me, axis, k):
    stride = (16, 4, 1)[axis]
    mine = lax.rem(lax.div(me, stride), 4)
    other = lax.rem(mine + k, 4)
    return me + (other - mine) * stride, mine, other


def greet(me, core):
    bar = pltpu.get_barrier_semaphore()
    for axis in range(3):
        for k in (1, 2, 3):
            p, _, _ = peer_of(me, axis, k)
            pl.semaphore_signal(bar, inc=1, device_id=(p, core), device_id_type=MESH)
    pl.semaphore_signal(bar, inc=1, device_id=(me, 1 - core), device_id_type=MESH)
    pl.semaphore_wait(bar, 10)


def eye(h):
    return lax.broadcasted_iota(jnp.int32, (h, 128), 0) == lax.broadcasted_iota(
        jnp.int32, (h, 128), 1
    )


def to_lanes(x):
    n = x.shape[0]
    sums = jnp.sum(x, axis=1, keepdims=True)
    rows = []
    for b in range(0, n, 128):
        h = min(128, n - b)
        rows.append(jnp.sum(jnp.where(eye(h), sums[b : b + h], 0.0), axis=0, keepdims=True))
    return jnp.concatenate(rows, axis=0)


def to_sublanes(row, h):
    return jnp.sum(jnp.where(eye(h), row, 0.0), axis=1, keepdims=True)


def combined_t(w, q, p, start, n):
    upd = lax.dot_general(
        q[:, pl.ds(start, n)], p, (((0,), (1,)), ((), ())), preferred_element_type=F32
    )
    return w[pl.ds(start, n), :].astype(F32) + upd


def at(ref, axis, idx, rows):
    ix = [slice(None)] * 3
    ix[axis] = idx
    return ref.at[(*ix, pl.ds(*rows))]


def merge_kernel(
    wg, wu, wd, qg, qu, qd, pg, pu, pd, mags,
    og, ou, od, s1g, s1u, s1d,
    vg, vu, vd, rg, ru, rd, sg, su, sd, s2g, s2u, s2d,
    full, turn, both_g, both_u, both_d, pdown, mag, sums, got, scale,
    w_sem, q_sem, p_send, p_recv, p_loc, r_send, r_recv, x_send, x_recv, x_loc,
):
    me = lax.axis_index("row")
    core = lax.axis_index("col")
    half = 7 * BLK
    w_parts = (pl.ds(0, half), pl.ds(half, COLS - half))
    w_load, q_load = [], []
    for i, (src, dst) in enumerate(((qg, rg), (wg, vg), (qu, ru), (wu, vu), (qd, rd), (wd, vd))):
        if i % 2 == 0:
            cp = pltpu.make_async_copy(src, dst, q_sem.at[i // 2])
            cp.start()
            q_load.append(cp)
        elif i < 5:
            cps = [
                pltpu.make_async_copy(src.at[part], dst.at[part], w_sem.at[i // 2, h])
                for h, part in enumerate(w_parts)
            ]
            for cp in cps:
                cp.start()
            w_load.append(cps)
        else:
            cp = pltpu.make_async_copy(src, dst, w_sem.at[2, 0])
            cp.start()
            w_load.append([cp])
    mag_load = pltpu.make_async_copy(mags, mag, q_sem.at[3])
    mag_load.start()
    greet(me, core)
    ps = []
    for i, (src, dst) in enumerate(((pg, both_g), (pu, both_u), (pd, both_d))):
        far = pltpu.make_async_remote_copy(
            src_ref=src, dst_ref=dst.at[core], send_sem=p_send.at[i], recv_sem=p_recv.at[i],
            device_id=(me, 1 - core), device_id_type=MESH,
        )
        near = pltpu.make_async_copy(src, dst.at[core], p_loc.at[i])
        far.start()
        near.start()
        ps.append((far, near))
    for far, near in ps:
        near.wait()
        far.wait()

    def sum_copy(i, ph, t, k):
        q, _, _ = peer_of(me, ORDERS[t][ph], k)
        rows = pl.ds(*SUM_ROWS[i][t])
        return pltpu.make_async_remote_copy(
            src_ref=sums.at[ph, rows], dst_ref=got.at[ph, k - 1, rows],
            send_sem=r_send.at[i, ph, t, k - 1], recv_sem=r_recv.at[i, ph, t, k - 1],
            device_id=(q, core), device_id_type=MESH,
        )

    def send_sums(i, ph):
        for t in range(3):
            for k in (2, 1, 3):
                sum_copy(i, ph, t, k).start()

    def take_sums(i, ph):
        for t in range(3):
            for k in (2, 1, 3):
                sum_copy(i, ph, t, k).wait_recv()
            rows = pl.ds(*SUM_ROWS[i][t])
            total = sums[ph, rows, :] + got[ph, 0, rows, :] + got[ph, 1, rows, :] + got[ph, 2, rows, :]
            if ph < 2:
                sums[ph + 1, rows, :] = total
            else:
                scale[rows, :] = mag[rows, :] / jnp.sqrt(total + EPS)

    stages = ((sg, s1g, s2g, og), (su, s1u, s2u, ou), (sd, s1d, s2d, od))

    def far_copy(g, ph, t, k):
        m, thirds = GROUPS[g]
        axis = ORDERS[t][ph]
        p, mine, other = peer_of(me, axis, k)
        return pltpu.make_async_remote_copy(
            src_ref=at(stages[m][ph], axis, other, thirds[t]),
            dst_ref=at(stages[m][ph + 1], axis, mine, thirds[t]),
            send_sem=x_send.at[g, ph, t, k - 1], recv_sem=x_recv.at[g, ph, t, k - 1],
            device_id=(p, core), device_id_type=MESH,
        )

    def near_copy(g, ph, t):
        m, thirds = GROUPS[g]
        axis = ORDERS[t][ph]
        _, mine, _ = peer_of(me, axis, 1)
        return pltpu.make_async_copy(
            at(stages[m][ph], axis, mine, thirds[t]),
            at(stages[m][ph + 1], axis, mine, thirds[t]),
            x_loc.at[g, ph, t],
        )

    def arrive(g, ph, t):
        for k in (2, 1, 3):
            far_copy(g, ph, t, k).wait_recv()
        near_copy(g, ph, t).wait()

    def send(g, ph):
        for t in range(3):
            if ph > 0:
                arrive(g, ph - 1, t)
            for k in (2, 1, 3):
                far_copy(g, ph, t, k).start()
            near_copy(g, ph, t).start()

    weights = ((vg, rg, both_g, sg), (vu, ru, both_u, su))
    blocks = COLS // BLK
    tail = blocks * BLK

    def square_blocks(i, lo, hi, last, keep):
        w, q, both, _ = weights[i]
        p = both[...].reshape(2 * RANK, RANK)

        def body(b, carry):
            start = pl.multiple_of(b * BLK, BLK)
            x = combined_t(w, q, p, start, BLK)
            if keep:
                full[pl.ds(start, BLK), :] = x
            sums[0, pl.ds(pl.multiple_of(FIRST[i] + b * 8, 8), 8), :] = to_lanes(x * x)
            return carry

        lax.fori_loop(lo, hi, body, 0)
        if last:
            x = combined_t(w, q, p, tail, COLS - tail)
            if keep:
                full[tail:COLS, :] = x
            sums[0, FIRST[i] + 112 : FIRST[i] + 116, :] = to_lanes(x * x)
            sums[0, FIRST[i] + 116 : FIRST[i] + 120, :] = jnp.zeros((4, 128), F32)

    def scale_blocks(i, kept):
        w, q, both, _ = weights[i]
        p = both[...].reshape(2 * RANK, RANK)

        def body(b, carry):
            start = pl.multiple_of(b * BLK, BLK)
            x = full[pl.ds(start, BLK), :] if kept else combined_t(w, q, p, start, BLK)
            f = scale[pl.ds(pl.multiple_of(FIRST[i] + b * 8, 8), 8), :]
            for e in range(8):
                full[pl.ds(pl.multiple_of(start + e * 128, 128), 128), :] = x[
                    e * 128 : (e + 1) * 128
                ] * to_sublanes(f[e : e + 1], 128)
            return carry

        lax.fori_loop(0, blocks, body, 0)
        x = full[tail:COLS, :] if kept else combined_t(w, q, p, tail, COLS - tail)
        f = scale[FIRST[i] + 112 : FIRST[i] + 116, :]
        for e in range(4):
            h = 128 if e < 3 else 64
            full[tail + e * 128 : tail + e * 128 + h, :] = x[
                e * 128 : e * 128 + h
            ] * to_sublanes(f[e : e + 1], h)

    def cut(i):
        s = weights[i][3]

        def body(g, carry):
            base = pl.multiple_of(g * (8 * SLAB), 8)
            for e in range(8):
                s[lax.div(g, 2), lax.rem(g, 2) * 2 + e // 4, e % 4] = full[
                    pl.ds(base + e * SLAB, SLAB + 1), :
                ].astype(BF)
            return carry

        lax.fori_loop(0, N // 8, body, 0)

    def down_block(j):
        lanes = pl.ds(pl.multiple_of(j * 128, 128), 128)
        p = pdown[0:DROWS, :].astype(BF)
        upd = jnp.dot(p, rd[:, lanes], preferred_element_type=F32)
        return vd[:, lanes].astype(F32) + upd

    def square_down(j, carry):
        x = down_block(j)
        sums[0, pl.ds(FIRST[2] + j, 1), :] = jnp.sum(x * x, axis=0, keepdims=True)
        return carry

    first = WINDOW - lax.rem(me * DROWS, WINDOW)

    def merge_down(j, carry):
        y = down_block(j) * scale[pl.ds(FIRST[2] + j, 1), :]
        turn[0:DROWS, :] = y
        turn[WINDOW : WINDOW + DROWS, :] = y
        z = turn[pl.ds(first, WINDOW), :].T.astype(BF)
        a, b, c = lax.div(j, 8), lax.rem(lax.div(j, 2), 4), lax.rem(j, 2) * 2
        for e in range(4):
            sd[a, b, c, e * 64 : (e + 1) * 64, :] = z[0:64, e * 128 : (e + 1) * 128]
            sd[a, b, c + 1, e * 64 : (e + 1) * 64, :] = z[64:128, e * 128 : (e + 1) * 128]
        return carry

    full[COLS : COLS + 8, :] = jnp.zeros((8, 128), F32)
    turn[...] = jnp.zeros_like(turn)
    q_load[0].wait()
    w_load[0][0].wait()
    square_blocks(0, 0, 7, False, True)
    w_load[0][1].wait()
    square_blocks(0, 7, blocks, True, True)
    send_sums(0, 0)
    q_load[1].wait()
    w_load[1][0].wait()
    square_blocks(1, 0, 7, False, False)
    take_sums(0, 0)
    send_sums(0, 1)
    w_load[1][1].wait()
    square_blocks(1, 7, blocks, True, False)
    take_sums(0, 1)
    send_sums(0, 2)
    send_sums(1, 0)
    pdown[0:231, :] = both_d[0].astype(F32).T
    pdown[231:462, :] = both_d[1].astype(F32).T
    q_load[2].wait()
    w_load[2][0].wait()
    lax.fori_loop(0, 12, square_down, 0)
    mag_load.wait()
    take_sums(0, 2)
    take_sums(1, 0)
    send_sums(1, 1)
    scale_blocks(0, True)
    take_sums(1, 1)
    send_sums(1, 2)
    cut(0)
    send(0, 0)
    lax.fori_loop(12, DCOLS // 128, square_down, 0)
    send_sums(2, 0)
    take_sums(1, 2)
    scale_blocks(1, False)
    cut(1)
    send(1, 0)
    take_sums(2, 0)
    send_sums(2, 1)
    send(0, 1)
    take_sums(2, 1)
    send_sums(2, 2)
    send(1, 1)
    send(0, 2)
    take_sums(2, 2)
    lax.fori_loop(0, DCOLS // 128, merge_down, 0)
    send(2, 0)
    send(3, 0)
    send(1, 2)
    for ph in (1, 2):
        send(2, ph)
        send(3, ph)
    for g in range(4):
        for t in range(3):
            arrive(g, 2, t)
    for g in range(4):
        for ph in range(3):
            for t in range(3):
                for k in (1, 2, 3):
                    far_copy(g, ph, t, k).wait_send()
    for i in range(3):
        for ph in range(3):
            for t in range(3):
                for k in (1, 2, 3):
                    sum_copy(i, ph, t, k).wait_send()


def merge(wg, wu, wd, qg, qu, qd, pg, pu, pd, mags):
    hbm = pl.BlockSpec(memory_space=pl.ANY)
    vmem = pl.BlockSpec(memory_space=pltpu.VMEM)
    slab = (4, 4, 4, SLAB + 1, 128)
    dslab = (4, 4, 4, 256, 128)
    shapes = (slab, slab, dslab)
    dma = pltpu.SemaphoreType.DMA
    return pl.pallas_call(
        merge_kernel,
        out_shape=[pltpu.VMEM(s, BF) for s in shapes]
        + [jax.ShapeDtypeStruct(s, BF) for s in shapes],
        in_specs=[hbm] * 6 + [vmem] * 3 + [hbm],
        out_specs=[vmem] * 3 + [hbm] * 3,
        scratch_shapes=[
            pltpu.VMEM((COLS, 128), BF), pltpu.VMEM((COLS, 128), BF),
            pltpu.VMEM((DROWS, DCOLS), BF),
            pltpu.VMEM((RANK, COLS), BF), pltpu.VMEM((RANK, COLS), BF),
            pltpu.VMEM((RANK, DCOLS), BF),
            *[pltpu.VMEM(s, BF) for s in shapes * 2],
            pltpu.VMEM((COLS + 8, 128), F32), pltpu.VMEM((2 * WINDOW, 128), F32),
            pltpu.VMEM((2, 64, 64), BF), pltpu.VMEM((2, 64, 64), BF), pltpu.VMEM((2, 64, 231), BF),
            pltpu.VMEM((464, 64), F32), pltpu.VMEM((272, 128), F32),
            pltpu.VMEM((3, 272, 128), F32), pltpu.VMEM((3, 3, 272, 128), F32),
            pltpu.VMEM((272, 128), F32),
            dma((3, 2)), dma((4,)), dma((3,)), dma((3,)), dma((3,)),
            dma((3, 3, 3, 3)), dma((3, 3, 3, 3)),
            dma((4, 3, 3, 3)), dma((4, 3, 3, 3)), dma((4, 3, 3)),
        ],
        compiler_params=pltpu.CompilerParams(
            collective_id=0, has_side_effects=True, vmem_limit_bytes=52 * 10**6
        ),
        name="merge",
    )(wg, wu, wd, qg, qu, qd, pg, pu, pd, mags)[:3]


def join_kernel(x, o):
    first = pl.program_id(0) * 8
    for e in range(8):
        o[:, e * 128 : (e + 1) * 128] = x[first + e, 0:SLAB, :]


def join(x):
    return pl.pallas_call(
        join_kernel,
        grid=(N // 8,),
        out_shape=jax.ShapeDtypeStruct((SLAB, N * 128), BF),
        in_specs=[pl.BlockSpec(memory_space=pltpu.VMEM)],
        out_specs=pl.BlockSpec((SLAB, 1024), lambda i: (0, i)),
        compiler_params=pltpu.CompilerParams(vmem_limit_bytes=16 * 2**20),
        name="join",
    )(x.reshape(N, SLAB + 1, 128))


TILES = 33


def join_down_kernel(x, o):
    g = pl.program_id(0)

    def tile(i, carry):
        t = g * TILES + i
        s = lax.div(t * 128, DROWS)
        nxt = jnp.minimum(s + 1, N - 1)
        rows = pl.ds(pl.multiple_of(lax.rem(t, 4) * 64, 64), 64)
        lane = t * 128 + lax.broadcasted_iota(jnp.int32, (64, 128), 1)
        a = x[s, rows, :]
        b = x[nxt, rows, :]
        o[:, pl.ds(pl.multiple_of(i * 128, 128), 128)] = jnp.where(lane < (s + 1) * DROWS, a, b)
        return carry

    lax.fori_loop(0, TILES, tile, 0)


def join_down(x):
    return pl.pallas_call(
        join_down_kernel,
        grid=(7,),
        out_shape=jax.ShapeDtypeStruct((64, 29568), BF),
        in_specs=[pl.BlockSpec(memory_space=pltpu.VMEM)],
        out_specs=pl.BlockSpec((64, TILES * 128), lambda i: (0, i)),
        compiler_params=pltpu.CompilerParams(vmem_limit_bytes=16 * 2**20),
        name="join_down",
    )(x.reshape(N, 256, 128))


def local(wg, wu, wd, pg, qg, pu, qu, pd, qd, mg, mu, md):
    pad = jnp.zeros((15360 - COLS,), F32)
    mags = jnp.concatenate((mg, pad, mu, pad, md)).reshape(272, 128)
    g, u, d = merge(wg.T, wu.T, wd, qg, qu, qd, pg, pu, pd.T, mags)
    return join(g).T, join(u).T, join_down(d).T


def solution(mesh):
    placed = (
        P("row", "col"),
        P("row", "col"),
        P("row", "col"),
        P(("row", "col"), None),
        P(None, "col"),
        P(("row", "col"), None),
        P(None, "col"),
        P(("row", "col"), None),
        P(None, "col"),
        P("col"),
        P("col"),
        P("col"),
    )
    return jax.shard_map(
        local,
        mesh=mesh,
        in_specs=placed,
        out_specs=(P(None, ("col", "row")), P(None, ("col", "row")), P(None, ("col", "row"))),
        check_vma=False,
    )
```

```python
import functools

import jax
import jax.numpy as jnp
from jax import lax
from jax.experimental import pallas as pl
from jax.experimental.pallas import tpu as pltpu
from jax.sharding import PartitionSpec as P

MESH = pl.DeviceIdType.MESH
BF = jnp.bfloat16
F32 = jnp.float32
EPS = 1e-06
RANK = 64
N = 64
COLS = 14784
SLAB = 231
DROWS = 462
DCOLS = 4096
WINDOW = 512
WIDE = 240
BLK = 1024
HALF = 8 * BLK
ORDERS = ((2, 1, 0), (1, 0, 2), (0, 2, 1))
FIRST = (0, 120, 240)
SUM_ROWS = (
    None,
    ((120, 40), (160, 40), (200, 40)),
    ((240, 8), (248, 8), (256, 16)),
)
GROUPS = (
    (0, ((0, 48), (80, 48), (160, 48))),
    (0, ((48, 32), (128, 32), (208, 32))),
    (1, ((0, 48), (80, 48), (160, 48))),
    (1, ((48, 32), (128, 32), (208, 24))),
    (2, ((0, 48), (80, 48), (176, 48))),
    (2, ((48, 32), (128, 48), (224, 32))),
)
P_ROWS = ((0, 32), (32, 16), (48, 16))


def peer_of(me, axis, k):
    stride = (16, 4, 1)[axis]
    mine = lax.rem(lax.div(me, stride), 4)
    other = lax.rem(mine + k, 4)
    return me + (other - mine) * stride, mine, other


def greet(me, core):
    bar = pltpu.get_barrier_semaphore()
    for axis in range(3):
        for k in (1, 2, 3):
            p, _, _ = peer_of(me, axis, k)
            pl.semaphore_signal(bar, inc=1, device_id=(p, core), device_id_type=MESH)
    pl.semaphore_signal(bar, inc=1, device_id=(me, 1 - core), device_id_type=MESH)
    pl.semaphore_wait(bar, 10)


def eye(h):
    return lax.broadcasted_iota(jnp.int32, (h, 128), 0) == lax.broadcasted_iota(
        jnp.int32, (h, 128), 1
    )


def to_lanes(x):
    n = x.shape[0]
    sums = jnp.sum(x, axis=1, keepdims=True)
    rows = []
    for b in range(0, n, 128):
        h = min(128, n - b)
        rows.append(jnp.sum(jnp.where(eye(h), sums[b : b + h], 0.0), axis=0, keepdims=True))
    return jnp.concatenate(rows, axis=0)


def to_sublanes(row, h):
    return jnp.sum(jnp.where(eye(h), row, 0.0), axis=1, keepdims=True)


def combined_t(w, q, p, start, n):
    upd = lax.dot_general(
        q[:, pl.ds(start, n)], p, (((0,), (1,)), ((), ())), preferred_element_type=F32
    )
    return w[pl.ds(start, n), :].astype(F32) + upd


def at(ref, axis, idx, rows):
    ix = [slice(None)] * 3
    ix[axis] = idx
    return ref.at[(*ix, pl.ds(*rows))]


def window(s):
    return jnp.minimum(lax.div(s * SLAB, 8) * 8, COLS - WIDE)


def merge_kernel(
    wg, wu, wd, qg, qu, qd, pg, pu, pd, mags,
    og, ou, od, s1u, s1d,
    vu, vd, rg, ru, rd, su, sd, s1g, s2g, s3g, s2u, s2d,
    full, turn, both_g, both_u, both_d, pdown, mag, sums, got, scale,
    gathered, qwin, qcol, mcol, acc, shift,
    w_sem, q_sem, p_send, p_recv, p_loc, r_send, r_recv, x_send, x_recv, x_loc,
    g_send, g_recv,
):
    me = lax.axis_index("row")
    core = lax.axis_index("col")
    mine_at = (lax.div(me, 16), lax.rem(lax.div(me, 4), 4), lax.rem(me, 4))
    half = 7 * BLK
    u_loads = [
        pltpu.make_async_copy(wu.at[part], vu.at[part], w_sem.at[h])
        for h, part in enumerate((pl.ds(0, half), pl.ds(half, COLS - half)))
    ]
    d_load = pltpu.make_async_copy(wd, vd, w_sem.at[2])
    q_loads = [
        pltpu.make_async_copy(src, dst, q_sem.at[i])
        for i, (src, dst) in enumerate(((qg, rg), (qu, ru), (qd, rd), (mags, mag)))
    ]
    q_loads[1].start()
    u_loads[0].start()
    greet(me, core)
    ps = []
    for i, (src, dst) in enumerate(((pg, both_g), (pu, both_u), (pd, both_d))):
        far = pltpu.make_async_remote_copy(
            src_ref=src, dst_ref=dst.at[core], send_sem=p_send.at[i], recv_sem=p_recv.at[i],
            device_id=(me, 1 - core), device_id_type=MESH,
        )
        near = pltpu.make_async_copy(src, dst.at[core], p_loc.at[i])
        far.start()
        near.start()
        ps.append((far, near))

    def sum_copy(i, ph, t, k):
        q, _, _ = peer_of(me, ORDERS[t][ph], k)
        rows = pl.ds(*SUM_ROWS[i][t])
        return pltpu.make_async_remote_copy(
            src_ref=sums.at[ph, rows], dst_ref=got.at[ph, k - 1, rows],
            send_sem=r_send.at[i, ph, t, k - 1], recv_sem=r_recv.at[i, ph, t, k - 1],
            device_id=(q, core), device_id_type=MESH,
        )

    def send_sums(i, ph):
        for t in range(3):
            for k in (2, 1, 3):
                sum_copy(i, ph, t, k).start()

    def take_sums(i, ph):
        for t in range(3):
            for k in (2, 1, 3):
                sum_copy(i, ph, t, k).wait_recv()
            rows = pl.ds(*SUM_ROWS[i][t])
            total = sums[ph, rows, :] + got[ph, 0, rows, :] + got[ph, 1, rows, :] + got[ph, 2, rows, :]
            if ph < 2:
                sums[ph + 1, rows, :] = total
            else:
                scale[rows, :] = mag[rows, :] / jnp.sqrt(total + EPS)

    stages = ((s1g, s1g, s2g, s3g), (su, s1u, s2u, ou), (sd, s1d, s2d, od))

    def far_copy(g, ph, t, k):
        m, thirds = GROUPS[g]
        axis = ORDERS[t][ph]
        p, mine, other = peer_of(me, axis, k)
        return pltpu.make_async_remote_copy(
            src_ref=at(stages[m][ph], axis, other, thirds[t]),
            dst_ref=at(stages[m][ph + 1], axis, mine, thirds[t]),
            send_sem=x_send.at[g, ph, t, k - 1], recv_sem=x_recv.at[g, ph, t, k - 1],
            device_id=(p, core), device_id_type=MESH,
        )

    def near_copy(g, ph, t):
        m, thirds = GROUPS[g]
        axis = ORDERS[t][ph]
        _, mine, _ = peer_of(me, axis, 1)
        return pltpu.make_async_copy(
            at(stages[m][ph], axis, mine, thirds[t]),
            at(stages[m][ph + 1], axis, mine, thirds[t]),
            x_loc.at[g, ph, t],
        )

    def arrive(g, ph, t):
        for k in (2, 1, 3):
            far_copy(g, ph, t, k).wait_recv()
        near_copy(g, ph, t).wait()

    def send(g, ph):
        for t in range(3):
            if ph > 0:
                arrive(g, ph - 1, t)
            for k in (2, 1, 3):
                far_copy(g, ph, t, k).start()
            near_copy(g, ph, t).start()

    def send_gate(g):
        for t, rows in enumerate(GROUPS[g][1]):
            axis = ORDERS[t][0]

            def place(i, value, axis=axis):
                ix = [lax.div(i, 4), lax.rem(i, 4)]
                ix.insert(axis, value)
                return ix

            def src(i, value, rows=rows, place=place):
                z, y, x = place(i, value)
                start = window(z * 16 + y * 4 + x) + rows[0]
                return wg.at[pl.ds(pl.multiple_of(start, 8), rows[1])]

            def go(i, carry, axis=axis, rows=rows, place=place, src=src, t=t):
                for k in (2, 1, 3):
                    p, mine, other = peer_of(me, axis, k)
                    pltpu.make_async_remote_copy(
                        src_ref=src(i, other),
                        dst_ref=s1g.at[(*place(i, mine), pl.ds(*rows))],
                        send_sem=x_send.at[g, 0, t, k - 1], recv_sem=x_recv.at[g, 0, t, k - 1],
                        device_id=(p, core), device_id_type=MESH,
                    ).start()
                _, mine, _ = peer_of(me, axis, 1)
                pltpu.make_async_copy(
                    src(i, mine), s1g.at[(*place(i, mine), pl.ds(*rows))], x_loc.at[g, 0, t]
                ).start()
                return carry

            lax.fori_loop(0, 16, go, 0)

    def factor_copy(ph, t, k):
        axis = ORDERS[t][ph]
        p, _, _ = peer_of(me, axis, k)
        ix = list(mine_at)
        for done in ORDERS[t][:ph]:
            ix[done] = slice(None)
        block = gathered.at[(*ix, pl.ds(*P_ROWS[t]))]
        return pltpu.make_async_remote_copy(
            src_ref=block, dst_ref=block,
            send_sem=g_send.at[ph, t, k - 1], recv_sem=g_recv.at[ph, t, k - 1],
            device_id=(p, core), device_id_type=MESH,
        )

    def send_factor(ph):
        for t in range(3):
            for k in (2, 1, 3):
                factor_copy(ph, t, k).start()

    def take_factor(ph):
        for t in range(3):
            for k in (2, 1, 3):
                factor_copy(ph, t, k).wait_recv()

    def source(i):
        return lax.div(i, 16), lax.rem(lax.div(i, 4), 4), lax.rem(i, 4)

    start = window(me)
    tile = lax.div(start, 128)
    inner = pl.multiple_of(start - tile * 128, 8)
    skip = me * SLAB - start

    def own_columns():
        @pl.when(me < N - 1)
        def _():
            qwin[...] = rg[:, pl.ds(pl.multiple_of(tile * 128, 128), 384)].astype(F32).T

        @pl.when(me == N - 1)
        def _():
            qwin[0:320, :] = rg[:, COLS - 320 : COLS].astype(F32).T

        qcol[...] = qwin[pl.ds(inner, WIDE), :].astype(BF)
        for e in range(3):
            mcol[e * 128 : (e + 1) * 128, :] = jnp.broadcast_to(
                to_sublanes(mag[pl.ds(tile + e, 1), :], 128), (128, 128)
            )

    def gate_block(i):
        z, y, x = source(i)
        upd = jnp.dot(qcol[...], gathered[z, y, x], preferred_element_type=F32)
        return s3g[z, y, x].astype(F32) + upd

    def gate_squares(i, carry):
        x = gate_block(i)
        acc[...] += x * x
        return carry

    def gate_scale():
        total = jnp.sum(acc[...], axis=1, keepdims=True)
        acc[...] = mcol[pl.ds(inner, WIDE), :] / jnp.sqrt(total + EPS)

    def gate_finish(i, carry):
        shift[0:WIDE, :] = gate_block(i) * acc[...]
        og[:, pl.ds(pl.multiple_of(i * 128, 128), 128)] = shift[pl.ds(skip, SLAB), :].astype(BF)
        return carry

    blocks = COLS // BLK
    tail = blocks * BLK

    def square_blocks(lo, hi, last):
        p = both_u[...].reshape(2 * RANK, RANK)

        def body(b, carry):
            x = combined_t(vu, ru, p, pl.multiple_of(b * BLK, BLK), BLK)
            sums[0, pl.ds(pl.multiple_of(FIRST[1] + b * 8, 8), 8), :] = to_lanes(x * x)
            return carry

        lax.fori_loop(lo, hi, body, 0)
        if last:
            x = combined_t(vu, ru, p, tail, COLS - tail)
            sums[0, FIRST[1] + 112 : FIRST[1] + 116, :] = to_lanes(x * x)
            sums[0, FIRST[1] + 116 : FIRST[1] + 120, :] = jnp.zeros((4, 128), F32)

    def merge_up(h):
        p = both_u[...].reshape(2 * RANK, RANK)
        lo = 7 * h

        def body(b, carry):
            start = pl.multiple_of(b * BLK, BLK)
            x = combined_t(vu, ru, p, start, BLK)
            f = scale[pl.ds(pl.multiple_of(FIRST[1] + b * 8, 8), 8), :]
            for e in range(8):
                to = pl.multiple_of(start - lo * BLK + e * 128, 128)
                full[pl.ds(to, 128), :] = x[e * 128 : (e + 1) * 128] * to_sublanes(f[e : e + 1], 128)
            return carry

        lax.fori_loop(lo, 8 if h == 0 else blocks, body, 0)
        if h == 1:
            x = combined_t(vu, ru, p, tail, COLS - tail)
            f = scale[FIRST[1] + 112 : FIRST[1] + 116, :]
            for e in range(4):
                n = 128 if e < 3 else 64
                to = tail - lo * BLK + e * 128
                full[to : to + n, :] = x[e * 128 : e * 128 + n] * to_sublanes(f[e : e + 1], n)
            end = COLS - lo * BLK
            full[end : end + 8, :] = jnp.zeros((8, 128), F32)

        def cut(g, carry):
            base = pl.multiple_of(g * (8 * SLAB) - lo * BLK, 8)
            for e in range(8):
                su[lax.div(g, 2), lax.rem(g, 2) * 2 + e // 4, e % 4] = full[
                    pl.ds(base + e * SLAB, SLAB + 1), :
                ].astype(BF)
            return carry

        lax.fori_loop(4 * h, 4 * h + 4, cut, 0)

    def down_block(j):
        lanes = pl.ds(pl.multiple_of(j * 128, 128), 128)
        p = pdown[0:DROWS, :].astype(BF)
        upd = jnp.dot(p, rd[:, lanes], preferred_element_type=F32)
        return vd[:, lanes].astype(F32) + upd

    def square_down(j, carry):
        x = down_block(j)
        sums[0, pl.ds(FIRST[2] + j, 1), :] = jnp.sum(x * x, axis=0, keepdims=True)
        return carry

    first = WINDOW - lax.rem(me * DROWS, WINDOW)

    def merge_down(j, carry):
        y = down_block(j) * scale[pl.ds(FIRST[2] + j, 1), :]
        turn[0:DROWS, :] = y
        turn[WINDOW : WINDOW + DROWS, :] = y
        z = turn[pl.ds(first, WINDOW), :].T.astype(BF)
        a, b, c = lax.div(j, 8), lax.rem(lax.div(j, 2), 4), lax.rem(j, 2) * 2
        for e in range(4):
            sd[a, b, c, e * 64 : (e + 1) * 64, :] = z[0:64, e * 128 : (e + 1) * 128]
            sd[a, b, c + 1, e * 64 : (e + 1) * 64, :] = z[64:128, e * 128 : (e + 1) * 128]
        return carry

    send_gate(0)
    send_gate(1)
    u_loads[1].start()
    q_loads[2].start()
    d_load.start()
    q_loads[3].start()
    q_loads[0].start()
    for far, near in ps:
        near.wait()
        far.wait()
    turn[...] = jnp.zeros_like(turn)
    acc[...] = jnp.zeros_like(acc)
    qwin[...] = jnp.zeros_like(qwin)
    gathered[mine_at] = both_g[...].reshape(2 * RANK, RANK).astype(F32).T.astype(BF)
    q_loads[1].wait()
    u_loads[0].wait()
    square_blocks(0, 7, False)
    send_factor(0)
    u_loads[1].wait()
    square_blocks(7, blocks, True)
    pdown[0:231, :] = both_d[0].astype(F32).T
    pdown[231:462, :] = both_d[1].astype(F32).T
    send_sums(1, 0)
    send(0, 1)
    q_loads[2].wait()
    d_load.wait()
    lax.fori_loop(0, 12, square_down, 0)
    take_factor(0)
    send_factor(1)
    q_loads[3].wait()
    take_sums(1, 0)
    send_sums(1, 1)
    send(1, 1)
    lax.fori_loop(12, DCOLS // 128, square_down, 0)
    send_sums(2, 0)
    take_sums(1, 1)
    send_sums(1, 2)
    send(0, 2)
    take_factor(1)
    send_factor(2)
    take_sums(1, 2)
    send(1, 2)
    merge_up(0)
    merge_up(1)
    take_sums(2, 0)
    send_sums(2, 1)
    send(2, 0)
    send(3, 0)
    q_loads[0].wait()
    own_columns()
    take_factor(2)
    for t in range(3):
        arrive(0, 2, t)
        arrive(1, 2, t)
    lax.fori_loop(0, N, gate_squares, 0)
    gate_scale()
    take_sums(2, 1)
    send_sums(2, 2)
    send(2, 1)
    lax.fori_loop(0, N, gate_finish, 0)
    send(3, 1)
    take_sums(2, 2)
    lax.fori_loop(0, DCOLS // 256, merge_down, 0)
    send(2, 2)
    lax.fori_loop(DCOLS // 256, DCOLS // 128, merge_down, 0)
    send(4, 0)
    send(5, 0)
    send(3, 2)
    for ph in (1, 2):
        send(4, ph)
        send(5, ph)
    for g in range(2, 6):
        for t in range(3):
            arrive(g, 2, t)
    for g in range(6):
        for ph in range(3):
            for t in range(3):
                for k in (1, 2, 3):
                    far_copy(g, ph, t, k).wait_send()
    for ph in range(3):
        for t in range(3):
            for k in (1, 2, 3):
                sum_copy(1, ph, t, k).wait_send()
                sum_copy(2, ph, t, k).wait_send()
                factor_copy(ph, t, k).wait_send()


def merge(wg, wu, wd, qg, qu, qd, pg, pu, pd, mags):
    hbm = pl.BlockSpec(memory_space=pl.ANY)
    vmem = pl.BlockSpec(memory_space=pltpu.VMEM)
    wide = (4, 4, 4, WIDE, 128)
    slab = (4, 4, 4, SLAB + 1, 128)
    dslab = (4, 4, 4, 256, 128)
    dma = pltpu.SemaphoreType.DMA
    return pl.pallas_call(
        merge_kernel,
        out_shape=[pltpu.VMEM(s, BF) for s in ((SLAB, N * 128), slab, dslab)]
        + [jax.ShapeDtypeStruct(s, BF) for s in (slab, dslab)],
        in_specs=[hbm] * 6 + [vmem] * 3 + [hbm],
        out_specs=[vmem] * 3 + [hbm] * 2,
        scratch_shapes=[
            pltpu.VMEM((COLS, 128), BF), pltpu.VMEM((DROWS, DCOLS), BF),
            pltpu.VMEM((RANK, COLS), BF), pltpu.VMEM((RANK, COLS), BF),
            pltpu.VMEM((RANK, DCOLS), BF),
            *[pltpu.VMEM(s, BF) for s in (slab, dslab, wide, wide, wide, slab, dslab)],
            pltpu.VMEM((HALF, 128), F32), pltpu.VMEM((2 * WINDOW, 128), F32),
            pltpu.VMEM((2, 64, 64), BF), pltpu.VMEM((2, 64, 64), BF), pltpu.VMEM((2, 64, 231), BF),
            pltpu.VMEM((464, 64), F32), pltpu.VMEM((272, 128), F32),
            pltpu.VMEM((3, 272, 128), F32), pltpu.VMEM((3, 3, 272, 128), F32),
            pltpu.VMEM((272, 128), F32),
            pltpu.VMEM((4, 4, 4, RANK, 128), BF), pltpu.VMEM((384, RANK), F32),
            pltpu.VMEM((WIDE, RANK), BF), pltpu.VMEM((384, 128), F32),
            pltpu.VMEM((WIDE, 128), F32), pltpu.VMEM((WIDE + 8, 128), F32),
            dma((3,)), dma((4,)), dma((3,)), dma((3,)), dma((3,)),
            dma((3, 3, 3, 3)), dma((3, 3, 3, 3)),
            dma((6, 3, 3, 3)), dma((6, 3, 3, 3)), dma((6, 3, 3)),
            dma((3, 3, 3)), dma((3, 3, 3)),
        ],
        compiler_params=pltpu.CompilerParams(
            collective_id=0, has_side_effects=True, vmem_limit_bytes=54 * 10**6
        ),
        name="merge",
    )(wg, wu, wd, qg, qu, qd, pg, pu, pd, mags)[:3]


LANES = 1024
TILES = 33
DEPTH = 4


def join_kernel(g, u, d, og, ou, od, bufs, dbufs, gsem, sem, dsem):
    gate = pltpu.make_async_copy(g, og, gsem)
    gate.start()

    def out_down(i):
        lanes = pl.ds(pl.multiple_of(i * (TILES * 128), 128), TILES * 128)
        b = lax.rem(i, DEPTH)
        return pltpu.make_async_copy(dbufs.at[b], od.at[:, lanes], dsem.at[b])

    def step_down(i, carry):
        @pl.when(i >= DEPTH)
        def _():
            out_down(i - DEPTH).wait()

        buf = dbufs.at[lax.rem(i, DEPTH)]

        def tile(j, carry):
            t = i * TILES + j
            s = lax.div(t * 128, DROWS)
            nxt = jnp.minimum(s + 1, N - 1)
            rows = pl.ds(pl.multiple_of(lax.rem(t, 4) * 64, 64), 64)
            lane = t * 128 + lax.broadcasted_iota(jnp.int32, (64, 128), 1)
            buf[:, pl.ds(pl.multiple_of(j * 128, 128), 128)] = jnp.where(
                lane < (s + 1) * DROWS, d[s, rows, :], d[nxt, rows, :]
            )
            return carry

        lax.fori_loop(0, TILES, tile, 0, unroll=11)
        out_down(i).start()
        return carry

    lax.fori_loop(0, 7, step_down, 0)

    def out(i):
        b = lax.rem(i, DEPTH)
        lanes = pl.ds(pl.multiple_of(i * LANES, LANES), LANES)
        return pltpu.make_async_copy(bufs.at[b], ou.at[:, lanes], sem.at[b])

    def step(i, carry):
        @pl.when(i >= DEPTH)
        def _():
            out(i - DEPTH).wait()

        buf = bufs.at[lax.rem(i, DEPTH)]
        for e in range(8):
            buf[:, e * 128 : (e + 1) * 128] = u[i * 8 + e, 0:SLAB, :]
        out(i).start()
        return carry

    lax.fori_loop(0, 8, step, 0)
    for n in range(3, 7):
        out_down(n).wait()
    for n in range(4, 8):
        out(n).wait()
    gate.wait()


def join(g, u, d):
    hbm = pl.BlockSpec(memory_space=pl.ANY)
    vmem = pl.BlockSpec(memory_space=pltpu.VMEM)
    dma = pltpu.SemaphoreType.DMA
    return pl.pallas_call(
        join_kernel,
        out_shape=[jax.ShapeDtypeStruct((SLAB, N * 128), BF)] * 2
        + [jax.ShapeDtypeStruct((64, N * DROWS), BF)],
        in_specs=[vmem] * 3,
        out_specs=[hbm] * 3,
        scratch_shapes=[
            pltpu.VMEM((DEPTH, SLAB, LANES), BF), pltpu.VMEM((DEPTH, 64, TILES * 128), BF),
            dma, dma((DEPTH,)), dma((DEPTH,)),
        ],
        compiler_params=pltpu.CompilerParams(vmem_limit_bytes=16 * 2**20),
        name="join",
    )(g, u.reshape(N, SLAB + 1, 128), d.reshape(N, 256, 128))


def local(wg, wu, wd, pg, qg, pu, qu, pd, qd, mg, mu, md):
    pad = jnp.zeros((15360 - COLS,), F32)
    mags = jnp.concatenate((mg, pad, mu, pad, md)).reshape(272, 128)
    g, u, d = merge(wg.T, wu.T, wd, qg, qu, qd, pg, pu, pd.T, mags)
    return tuple(o.T for o in join(g, u, d))


def solution(mesh):
    placed = (
        P("row", "col"),
        P("row", "col"),
        P("row", "col"),
        P(("row", "col"), None),
        P(None, "col"),
        P(("row", "col"), None),
        P(None, "col"),
        P(("row", "col"), None),
        P(None, "col"),
        P("col"),
        P("col"),
        P("col"),
    )
    return jax.shard_map(
        local,
        mesh=mesh,
        in_specs=placed,
        out_specs=(P(None, ("col", "row")), P(None, ("col", "row")), P(None, ("col", "row"))),
        check_vma=False,
    )
```

```python
import functools

import jax
import jax.numpy as jnp
from jax import lax
from jax.experimental import pallas as pl
from jax.experimental.pallas import tpu as pltpu
from jax.sharding import PartitionSpec as P

MESH = pl.DeviceIdType.MESH
BF = jnp.bfloat16
F32 = jnp.float32
EPS = 1e-06
RANK = 64
N = 64
COLS = 14784
SLAB = 231
DROWS = 462
DCOLS = 4096
WINDOW = 512
WIDE = 240
BLK = 1024
HALF = 8 * BLK
ORDERS = ((2, 1, 0), (1, 0, 2), (0, 2, 1))
FIRST = (0, 120, 240)
SUM_ROWS = ((120, 48), (168, 56), (224, 48))
GROUPS = (
    (0, ((0, 48), (80, 48), (160, 48))),
    (0, ((48, 32), (128, 32), (208, 32))),
    (1, ((0, 48), (80, 48), (160, 48))),
    (1, ((48, 32), (128, 32), (208, 24))),
    (2, ((0, 48), (80, 48), (176, 48))),
    (2, ((48, 32), (128, 48), (224, 32))),
)
G_ROWS = ((0, 80), (80, 80), (160, 80))
P_ROWS = ((0, 32), (32, 16), (48, 16))


def peer_of(me, axis, k):
    stride = (16, 4, 1)[axis]
    mine = lax.rem(lax.div(me, stride), 4)
    other = lax.rem(mine + k, 4)
    return me + (other - mine) * stride, mine, other


def greet(me, core):
    bar = pltpu.get_barrier_semaphore()
    for axis in range(3):
        for k in (1, 2, 3):
            p, _, _ = peer_of(me, axis, k)
            pl.semaphore_signal(bar, inc=1, device_id=(p, core), device_id_type=MESH)
    pl.semaphore_signal(bar, inc=1, device_id=(me, 1 - core), device_id_type=MESH)
    pl.semaphore_wait(bar, 10)


def eye(h):
    return lax.broadcasted_iota(jnp.int32, (h, 128), 0) == lax.broadcasted_iota(
        jnp.int32, (h, 128), 1
    )


def to_lanes(x):
    n = x.shape[0]
    sums = jnp.sum(x, axis=1, keepdims=True)
    rows = []
    for b in range(0, n, 128):
        h = min(128, n - b)
        rows.append(jnp.sum(jnp.where(eye(h), sums[b : b + h], 0.0), axis=0, keepdims=True))
    return jnp.concatenate(rows, axis=0)


def to_sublanes(row, h):
    return jnp.sum(jnp.where(eye(h), row, 0.0), axis=1, keepdims=True)


def combined_t(w, q, p, start, n):
    upd = lax.dot_general(
        q[:, pl.ds(start, n)], p, (((0,), (1,)), ((), ())), preferred_element_type=F32
    )
    return w[pl.ds(start, n), :].astype(F32) + upd


def at(ref, axis, idx, rows):
    ix = [slice(None)] * 3
    ix[axis] = idx
    return ref.at[(*ix, pl.ds(*rows))]


def window(s):
    return jnp.minimum(lax.div(s * SLAB, 8) * 8, COLS - WIDE)


def merge_kernel(
    wg, wu, wd, qg, qu, qd, pg, pu, pd, mags,
    og, ou, od, s1u, s1d,
    vu, vd, rg, ru, rd, su, sd, s1g, s2g, s3g, s2u, s2d,
    full, turn, both_g, both_u, both_d, pdown, mag, sums, got, scale,
    gathered, qwin, qcol, mcol, acc, shift,
    w_sem, q_sem, p_send, p_recv, p_loc, r_send, r_recv, x_send, x_recv, x_loc,
    g_send, g_recv,
):
    me = lax.axis_index("row")
    core = lax.axis_index("col")
    mine_at = (lax.div(me, 16), lax.rem(lax.div(me, 4), 4), lax.rem(me, 4))
    half = 7 * BLK
    u_loads = [
        pltpu.make_async_copy(wu.at[part], vu.at[part], w_sem.at[h])
        for h, part in enumerate((pl.ds(0, half), pl.ds(half, COLS - half)))
    ]
    d_load = pltpu.make_async_copy(wd, vd, w_sem.at[2])
    q_loads = [
        pltpu.make_async_copy(src, dst, q_sem.at[i])
        for i, (src, dst) in enumerate(((qg, rg), (qu, ru), (qd, rd), (mags, mag)))
    ]
    q_loads[1].start()
    u_loads[0].start()
    greet(me, core)
    ps = []
    for i, (src, dst) in enumerate(((pg, both_g), (pu, both_u), (pd, both_d))):
        far = pltpu.make_async_remote_copy(
            src_ref=src, dst_ref=dst.at[core], send_sem=p_send.at[i], recv_sem=p_recv.at[i],
            device_id=(me, 1 - core), device_id_type=MESH,
        )
        near = pltpu.make_async_copy(src, dst.at[core], p_loc.at[i])
        far.start()
        near.start()
        ps.append((far, near))

    def sum_copy(ph, t, k):
        q, _, _ = peer_of(me, ORDERS[t][ph], k)
        rows = pl.ds(*SUM_ROWS[t])
        return pltpu.make_async_remote_copy(
            src_ref=sums.at[ph, rows], dst_ref=got.at[ph, k - 1, rows],
            send_sem=r_send.at[ph, t, k - 1], recv_sem=r_recv.at[ph, t, k - 1],
            device_id=(q, core), device_id_type=MESH,
        )

    def send_sums(ph):
        for t in range(3):
            for k in (2, 1, 3):
                sum_copy(ph, t, k).start()

    def take_sums(ph):
        for t in range(3):
            for k in (2, 1, 3):
                sum_copy(ph, t, k).wait_recv()
            rows = pl.ds(*SUM_ROWS[t])
            total = sums[ph, rows, :] + got[ph, 0, rows, :] + got[ph, 1, rows, :] + got[ph, 2, rows, :]
            if ph < 2:
                sums[ph + 1, rows, :] = total
            else:
                scale[rows, :] = mag[rows, :] / jnp.sqrt(total + EPS)

    stages = ((s1g, s1g, s2g, s3g), (su, s1u, s2u, ou), (sd, s1d, s2d, od))

    def far_copy(g, ph, t, k):
        m, thirds = GROUPS[g]
        if m == 0 and ph == 0:
            thirds = G_ROWS
        axis = ORDERS[t][ph]
        p, mine, other = peer_of(me, axis, k)
        return pltpu.make_async_remote_copy(
            src_ref=at(stages[m][ph], axis, other, thirds[t]),
            dst_ref=at(stages[m][ph + 1], axis, mine, thirds[t]),
            send_sem=x_send.at[g, ph, t, k - 1], recv_sem=x_recv.at[g, ph, t, k - 1],
            device_id=(p, core), device_id_type=MESH,
        )

    def near_copy(g, ph, t):
        m, thirds = GROUPS[g]
        if m == 0 and ph == 0:
            thirds = G_ROWS
        axis = ORDERS[t][ph]
        _, mine, _ = peer_of(me, axis, 1)
        return pltpu.make_async_copy(
            at(stages[m][ph], axis, mine, thirds[t]),
            at(stages[m][ph + 1], axis, mine, thirds[t]),
            x_loc.at[g, ph, t],
        )

    def arrive(g, ph, t):
        for k in (2, 1, 3):
            far_copy(g, ph, t, k).wait_recv()
        near_copy(g, ph, t).wait()

    def send(g, ph):
        for t in range(3):
            if ph > 0 and (g, ph) != (1, 1):
                arrive(g, ph - 1, t)
            for k in (2, 1, 3):
                far_copy(g, ph, t, k).start()
            near_copy(g, ph, t).start()

    def send_gate():
        sides = []
        for axis in range(3):
            stride = (16, 4, 1)[axis]
            for k in (2, 1, 3):
                p, mine, other = peer_of(me, axis, k)
                sides.append((axis, k, p, mine, other * stride))
            sides.append((axis, 0, None, mine, mine * stride))

        def go(i, carry):
            for e in range(4):
                for t, rows in enumerate(G_ROWS):
                    for axis, k, p, mine, base in sides:
                        if axis != ORDERS[t][0]:
                            continue
                        ix = [i, e]
                        ix.insert(axis, mine)
                        others = (i * 4 + e, i * 16 + e, i * 16 + e * 4)[axis]
                        start = pl.multiple_of(window(base + others) + rows[0], 8)
                        src = wg.at[pl.ds(start, rows[1])]
                        dst = s1g.at[(*ix, pl.ds(*rows))]
                        if k == 0:
                            pltpu.make_async_copy(src, dst, x_loc.at[0, 0, t]).start()
                        else:
                            pltpu.make_async_remote_copy(
                                src_ref=src, dst_ref=dst,
                                send_sem=x_send.at[0, 0, t, k - 1],
                                recv_sem=x_recv.at[0, 0, t, k - 1],
                                device_id=(p, core), device_id_type=MESH,
                            ).start()
            return carry

        lax.fori_loop(0, 4, go, 0)

    def factor_copy(ph, t, k):
        axis = ORDERS[t][ph]
        p, _, _ = peer_of(me, axis, k)
        ix = list(mine_at)
        for done in ORDERS[t][:ph]:
            ix[done] = slice(None)
        block = gathered.at[(*ix, pl.ds(*P_ROWS[t]))]
        return pltpu.make_async_remote_copy(
            src_ref=block, dst_ref=block,
            send_sem=g_send.at[ph, t, k - 1], recv_sem=g_recv.at[ph, t, k - 1],
            device_id=(p, core), device_id_type=MESH,
        )

    def send_factor(ph):
        for t in range(3):
            for k in (2, 1, 3):
                factor_copy(ph, t, k).start()

    def take_factor(ph):
        for t in range(3):
            for k in (2, 1, 3):
                factor_copy(ph, t, k).wait_recv()

    def source(i):
        return lax.div(i, 16), lax.rem(lax.div(i, 4), 4), lax.rem(i, 4)

    start = window(me)
    tile = lax.div(start, 128)
    inner = pl.multiple_of(start - tile * 128, 8)
    skip = me * SLAB - start

    def own_columns():
        @pl.when(me < N - 1)
        def _():
            qwin[...] = rg[:, pl.ds(pl.multiple_of(tile * 128, 128), 384)].astype(F32).T

        @pl.when(me == N - 1)
        def _():
            qwin[0:320, :] = rg[:, COLS - 320 : COLS].astype(F32).T

        qcol[...] = qwin[pl.ds(inner, WIDE), :].astype(BF)
        for e in range(3):
            mcol[e * 128 : (e + 1) * 128, :] = jnp.broadcast_to(
                to_sublanes(mag[pl.ds(tile + e, 1), :], 128), (128, 128)
            )

    def gate_block(i):
        z, y, x = source(i)
        upd = jnp.dot(qcol[...], gathered[z, y, x], preferred_element_type=F32)
        return s3g[z, y, x].astype(F32) + upd

    def gate_squares(i, carry):
        x = gate_block(i)
        acc[...] += x * x
        return carry

    def gate_scale():
        total = jnp.sum(acc[...], axis=1, keepdims=True)
        acc[...] = mcol[pl.ds(inner, WIDE), :] / jnp.sqrt(total + EPS)

    def gate_finish(i, carry):
        shift[0:WIDE, :] = gate_block(i) * acc[...]
        og[:, pl.ds(pl.multiple_of(i * 128, 128), 128)] = shift[pl.ds(skip, SLAB), :].astype(BF)
        return carry

    blocks = COLS // BLK
    tail = blocks * BLK

    def square_blocks(lo, hi, last):
        p = both_u[...].reshape(2 * RANK, RANK)

        def body(b, carry):
            x = combined_t(vu, ru, p, pl.multiple_of(b * BLK, BLK), BLK)
            sums[0, pl.ds(pl.multiple_of(FIRST[1] + b * 8, 8), 8), :] = to_lanes(x * x)
            return carry

        lax.fori_loop(lo, hi, body, 0)
        if last:
            x = combined_t(vu, ru, p, tail, COLS - tail)
            sums[0, FIRST[1] + 112 : FIRST[1] + 116, :] = to_lanes(x * x)
            sums[0, FIRST[1] + 116 : FIRST[1] + 120, :] = jnp.zeros((4, 128), F32)

    def merge_up(h):
        p = both_u[...].reshape(2 * RANK, RANK)
        lo = 7 * h

        def body(b, carry):
            start = pl.multiple_of(b * BLK, BLK)
            x = combined_t(vu, ru, p, start, BLK)
            f = scale[pl.ds(pl.multiple_of(FIRST[1] + b * 8, 8), 8), :]
            for e in range(8):
                to = pl.multiple_of(start - lo * BLK + e * 128, 128)
                full[pl.ds(to, 128), :] = x[e * 128 : (e + 1) * 128] * to_sublanes(f[e : e + 1], 128)
            return carry

        lax.fori_loop(lo, 8 if h == 0 else blocks, body, 0)
        if h == 1:
            x = combined_t(vu, ru, p, tail, COLS - tail)
            f = scale[FIRST[1] + 112 : FIRST[1] + 116, :]
            for e in range(4):
                n = 128 if e < 3 else 64
                to = tail - lo * BLK + e * 128
                full[to : to + n, :] = x[e * 128 : e * 128 + n] * to_sublanes(f[e : e + 1], n)
            end = COLS - lo * BLK
            full[end : end + 8, :] = jnp.zeros((8, 128), F32)

        def cut(g, carry):
            base = pl.multiple_of(g * (8 * SLAB) - lo * BLK, 8)
            for e in range(8):
                su[lax.div(g, 2), lax.rem(g, 2) * 2 + e // 4, e % 4] = full[
                    pl.ds(base + e * SLAB, SLAB + 1), :
                ].astype(BF)
            return carry

        lax.fori_loop(4 * h, 4 * h + 4, cut, 0)

    def down_block(j):
        lanes = pl.ds(pl.multiple_of(j * 128, 128), 128)
        p = pdown[0:DROWS, :].astype(BF)
        upd = jnp.dot(p, rd[:, lanes], preferred_element_type=F32)
        return vd[:, lanes].astype(F32) + upd

    def square_down(j, carry):
        x = down_block(j)
        sums[0, pl.ds(FIRST[2] + j, 1), :] = jnp.sum(x * x, axis=0, keepdims=True)
        return carry

    first = WINDOW - lax.rem(me * DROWS, WINDOW)

    def merge_down(j, carry):
        y = down_block(j) * scale[pl.ds(FIRST[2] + j, 1), :]
        turn[0:DROWS, :] = y
        turn[WINDOW : WINDOW + DROWS, :] = y
        z = turn[pl.ds(first, WINDOW), :].T.astype(BF)
        a, b, c = lax.div(j, 8), lax.rem(lax.div(j, 2), 4), lax.rem(j, 2) * 2
        for e in range(4):
            sd[a, b, c, e * 64 : (e + 1) * 64, :] = z[0:64, e * 128 : (e + 1) * 128]
            sd[a, b, c + 1, e * 64 : (e + 1) * 64, :] = z[64:128, e * 128 : (e + 1) * 128]
        return carry

    send_gate()
    u_loads[1].start()
    q_loads[2].start()
    d_load.start()
    q_loads[3].start()
    q_loads[0].start()
    for far, near in ps:
        near.wait()
        far.wait()
    turn[...] = jnp.zeros_like(turn)
    acc[...] = jnp.zeros_like(acc)
    qwin[...] = jnp.zeros_like(qwin)
    gathered[mine_at] = both_g[...].reshape(2 * RANK, RANK).astype(F32).T.astype(BF)
    q_loads[1].wait()
    u_loads[0].wait()
    square_blocks(0, 7, False)
    send_factor(0)
    u_loads[1].wait()
    square_blocks(7, blocks, True)
    pdown[0:231, :] = both_d[0].astype(F32).T
    pdown[231:462, :] = both_d[1].astype(F32).T
    q_loads[2].wait()
    d_load.wait()
    lax.fori_loop(0, DCOLS // 128, square_down, 0)
    send_sums(0)
    send(0, 1)
    q_loads[3].wait()
    take_sums(0)
    send_sums(1)
    send(1, 1)
    take_factor(0)
    send_factor(1)
    take_sums(1)
    send_sums(2)
    send(0, 2)
    take_sums(2)
    send(1, 2)
    merge_up(0)
    merge_up(1)
    send(2, 0)
    send(3, 0)
    take_factor(1)
    send_factor(2)
    lax.fori_loop(0, DCOLS // 256, merge_down, 0)
    send(2, 1)
    lax.fori_loop(DCOLS // 256, DCOLS // 128, merge_down, 0)
    send(3, 1)
    send(4, 0)
    send(2, 2)
    send(5, 0)
    q_loads[0].wait()
    own_columns()
    take_factor(2)
    for t in range(3):
        arrive(0, 2, t)
        arrive(1, 2, t)
    send(3, 2)
    lax.fori_loop(0, N // 2, gate_squares, 0)
    send(4, 1)
    lax.fori_loop(N // 2, N, gate_squares, 0)
    gate_scale()
    send(5, 1)
    lax.fori_loop(0, N // 2, gate_finish, 0)
    send(4, 2)
    lax.fori_loop(N // 2, N, gate_finish, 0)
    send(5, 2)
    for g in range(2, 6):
        for t in range(3):
            arrive(g, 2, t)
    for g in range(6):
        for ph in range(3):
            if (g, ph) == (1, 0):
                continue
            for t in range(3):
                for k in (1, 2, 3):
                    far_copy(g, ph, t, k).wait_send()
    for ph in range(3):
        for t in range(3):
            for k in (1, 2, 3):
                sum_copy(ph, t, k).wait_send()
                factor_copy(ph, t, k).wait_send()


def merge(wg, wu, wd, qg, qu, qd, pg, pu, pd, mags):
    hbm = pl.BlockSpec(memory_space=pl.ANY)
    vmem = pl.BlockSpec(memory_space=pltpu.VMEM)
    wide = (4, 4, 4, WIDE, 128)
    slab = (4, 4, 4, SLAB + 1, 128)
    dslab = (4, 4, 4, 256, 128)
    dma = pltpu.SemaphoreType.DMA
    return pl.pallas_call(
        merge_kernel,
        out_shape=[pltpu.VMEM(s, BF) for s in ((SLAB, N * 128), slab, dslab)]
        + [jax.ShapeDtypeStruct(s, BF) for s in (slab, dslab)],
        in_specs=[hbm] * 6 + [vmem] * 3 + [hbm],
        out_specs=[vmem] * 3 + [hbm] * 2,
        scratch_shapes=[
            pltpu.VMEM((COLS, 128), BF), pltpu.VMEM((DROWS, DCOLS), BF),
            pltpu.VMEM((RANK, COLS), BF), pltpu.VMEM((RANK, COLS), BF),
            pltpu.VMEM((RANK, DCOLS), BF),
            *[pltpu.VMEM(s, BF) for s in (slab, dslab, wide, wide, wide, slab, dslab)],
            pltpu.VMEM((HALF, 128), F32), pltpu.VMEM((2 * WINDOW, 128), F32),
            pltpu.VMEM((2, 64, 64), BF), pltpu.VMEM((2, 64, 64), BF), pltpu.VMEM((2, 64, 231), BF),
            pltpu.VMEM((464, 64), F32), pltpu.VMEM((272, 128), F32),
            pltpu.VMEM((3, 272, 128), F32), pltpu.VMEM((3, 3, 272, 128), F32),
            pltpu.VMEM((272, 128), F32),
            pltpu.VMEM((4, 4, 4, RANK, 128), BF), pltpu.VMEM((384, RANK), F32),
            pltpu.VMEM((WIDE, RANK), BF), pltpu.VMEM((384, 128), F32),
            pltpu.VMEM((WIDE, 128), F32), pltpu.VMEM((WIDE + 8, 128), F32),
            dma((3,)), dma((4,)), dma((3,)), dma((3,)), dma((3,)),
            dma((3, 3, 3)), dma((3, 3, 3)),
            dma((6, 3, 3, 3)), dma((6, 3, 3, 3)), dma((6, 3, 3)),
            dma((3, 3, 3)), dma((3, 3, 3)),
        ],
        compiler_params=pltpu.CompilerParams(
            collective_id=0, has_side_effects=True, vmem_limit_bytes=54 * 10**6
        ),
        name="merge",
    )(wg, wu, wd, qg, qu, qd, pg, pu, pd, mags)[:3]


LANES = 1024
TILES = 33
DEPTH = 4


def join_kernel(g, u, d, og, ou, od, bufs, dbufs, gsem, sem, dsem):
    gate = pltpu.make_async_copy(g, og, gsem)
    gate.start()

    def out_down(i):
        lanes = pl.ds(pl.multiple_of(i * (TILES * 128), 128), TILES * 128)
        b = lax.rem(i, DEPTH)
        return pltpu.make_async_copy(dbufs.at[b], od.at[:, lanes], dsem.at[b])

    def step_down(i, carry):
        @pl.when(i >= DEPTH)
        def _():
            out_down(i - DEPTH).wait()

        buf = dbufs.at[lax.rem(i, DEPTH)]

        def tile(j, carry):
            t = i * TILES + j
            s = lax.div(t * 128, DROWS)
            nxt = jnp.minimum(s + 1, N - 1)
            rows = pl.ds(pl.multiple_of(lax.rem(t, 4) * 64, 64), 64)
            lane = t * 128 + lax.broadcasted_iota(jnp.int32, (64, 128), 1)
            buf[:, pl.ds(pl.multiple_of(j * 128, 128), 128)] = jnp.where(
                lane < (s + 1) * DROWS, d[s, rows, :], d[nxt, rows, :]
            )
            return carry

        lax.fori_loop(0, TILES, tile, 0, unroll=11)
        out_down(i).start()
        return carry

    lax.fori_loop(0, 7, step_down, 0)

    def out(i):
        b = lax.rem(i, DEPTH)
        lanes = pl.ds(pl.multiple_of(i * LANES, LANES), LANES)
        return pltpu.make_async_copy(bufs.at[b], ou.at[:, lanes], sem.at[b])

    def step(i, carry):
        @pl.when(i >= DEPTH)
        def _():
            out(i - DEPTH).wait()

        buf = bufs.at[lax.rem(i, DEPTH)]
        for e in range(8):
            buf[:, e * 128 : (e + 1) * 128] = u[i * 8 + e, 0:SLAB, :]
        out(i).start()
        return carry

    lax.fori_loop(0, 8, step, 0)
    for n in range(3, 7):
        out_down(n).wait()
    for n in range(4, 8):
        out(n).wait()
    gate.wait()


def join(g, u, d):
    hbm = pl.BlockSpec(memory_space=pl.ANY)
    vmem = pl.BlockSpec(memory_space=pltpu.VMEM)
    dma = pltpu.SemaphoreType.DMA
    return pl.pallas_call(
        join_kernel,
        out_shape=[jax.ShapeDtypeStruct((SLAB, N * 128), BF)] * 2
        + [jax.ShapeDtypeStruct((64, N * DROWS), BF)],
        in_specs=[vmem] * 3,
        out_specs=[hbm] * 3,
        scratch_shapes=[
            pltpu.VMEM((DEPTH, SLAB, LANES), BF), pltpu.VMEM((DEPTH, 64, TILES * 128), BF),
            dma, dma((DEPTH,)), dma((DEPTH,)),
        ],
        compiler_params=pltpu.CompilerParams(vmem_limit_bytes=16 * 2**20),
        name="join",
    )(g, u.reshape(N, SLAB + 1, 128), d.reshape(N, 256, 128))


def local(wg, wu, wd, pg, qg, pu, qu, pd, qd, mg, mu, md):
    pad = jnp.zeros((15360 - COLS,), F32)
    mags = jnp.concatenate((mg, pad, mu, pad, md)).reshape(272, 128)
    g, u, d = merge(wg.T, wu.T, wd, qg, qu, qd, pg, pu, pd.T, mags)
    return tuple(o.T for o in join(g, u, d))


def solution(mesh):
    placed = (
        P("row", "col"),
        P("row", "col"),
        P("row", "col"),
        P(("row", "col"), None),
        P(None, "col"),
        P(("row", "col"), None),
        P(None, "col"),
        P(("row", "col"), None),
        P(None, "col"),
        P("col"),
        P("col"),
        P("col"),
    )
    return jax.shard_map(
        local,
        mesh=mesh,
        in_specs=placed,
        out_specs=(P(None, ("col", "row")), P(None, ("col", "row")), P(None, ("col", "row"))),
        check_vma=False,
    )
```

```python
import functools

import jax
import jax.numpy as jnp
from jax import lax
from jax.experimental import pallas as pl
from jax.experimental.pallas import tpu as pltpu
from jax.sharding import PartitionSpec as P

MESH = pl.DeviceIdType.MESH
BF = jnp.bfloat16
F32 = jnp.float32
EPS = 1e-06
RANK = 64
N = 64
COLS = 14784
SLAB = 231
DROWS = 462
DCOLS = 4096
WINDOW = 512
WIDE = 240
BLK = 1024
HALF = 8 * BLK
ORDERS = ((2, 1, 0), (1, 0, 2), (0, 2, 1))
FIRST = (0, 120, 240)
SUM_ROWS = ((120, 48), (168, 56), (224, 48))
GROUPS = (
    (0, ((0, 48), (80, 48), (160, 48))),
    (0, ((48, 32), (128, 32), (208, 32))),
    (1, ((0, 48), (80, 48), (160, 48))),
    (1, ((48, 32), (128, 32), (208, 24))),
    (2, ((0, 48), (80, 48), (176, 48))),
    (2, ((48, 32), (128, 48), (224, 32))),
)
G_ROWS = ((0, 80), (80, 80), (160, 80))
P_ROWS = ((0, 16), (16, 16))


def peer_of(me, axis, k):
    stride = (16, 4, 1)[axis]
    mine = lax.rem(lax.div(me, stride), 4)
    other = lax.rem(mine + k, 4)
    return me + (other - mine) * stride, mine, other


def greet(me, core):
    bar = pltpu.get_barrier_semaphore()
    for axis in range(3):
        for k in (1, 2, 3):
            p, _, _ = peer_of(me, axis, k)
            pl.semaphore_signal(bar, inc=1, device_id=(p, core), device_id_type=MESH)
    pl.semaphore_signal(bar, inc=1, device_id=(me, 1 - core), device_id_type=MESH)
    pl.semaphore_wait(bar, 10)


def eye(h):
    return lax.broadcasted_iota(jnp.int32, (h, 128), 0) == lax.broadcasted_iota(
        jnp.int32, (h, 128), 1
    )


def to_lanes(x):
    n = x.shape[0]
    sums = jnp.sum(x, axis=1, keepdims=True)
    rows = []
    for b in range(0, n, 128):
        h = min(128, n - b)
        rows.append(jnp.sum(jnp.where(eye(h), sums[b : b + h], 0.0), axis=0, keepdims=True))
    return jnp.concatenate(rows, axis=0)


def to_sublanes(row, h):
    return jnp.sum(jnp.where(eye(h), row, 0.0), axis=1, keepdims=True)


def combined_t(w, q, p, start, n):
    upd = lax.dot_general(
        q[:, pl.ds(start, n)], p, (((0,), (1,)), ((), ())), preferred_element_type=F32
    )
    return w[pl.ds(start, n), :].astype(F32) + upd


def at(ref, axis, idx, rows):
    ix = [slice(None)] * 3
    ix[axis] = idx
    return ref.at[(*ix, pl.ds(*rows))]


def window(s):
    return jnp.minimum(lax.div(s * SLAB, 8) * 8, COLS - WIDE)


def merge_kernel(
    wg, wu, wd, qg, qu, qd, pg, pu, pd, mg, mu, md,
    og, ou, od, s1u, s1d,
    vu, vd, rg, ru, rd, su, sd, s1g, s2g, s3g, s2u, s2d,
    full, turn, both_g, both_u, both_d, pdown, mag, sums, got, scale,
    gathered, qwin, qcol, mcol, acc, shift,
    w_sem, q_sem, p_send, p_recv, p_loc, r_send, r_recv, x_send, x_recv, x_loc,
    g_send, g_recv,
):
    me = lax.axis_index("row")
    core = lax.axis_index("col")
    mine_at = (lax.div(me, 16), lax.rem(lax.div(me, 4), 4), lax.rem(me, 4))
    half = 7 * BLK
    u_loads = [
        pltpu.make_async_copy(wu.at[part], vu.at[part], w_sem.at[h])
        for h, part in enumerate((pl.ds(0, half), pl.ds(half, COLS - half)))
    ]
    d_load = pltpu.make_async_copy(wd, vd, w_sem.at[2])
    q_loads = [
        pltpu.make_async_copy(src, dst, q_sem.at[i])
        for i, (src, dst) in enumerate(((qg, rg), (qu, ru), (qd, rd)))
    ]
    q_loads[1].start()
    u_loads[0].start()
    greet(me, core)
    ps = []
    for i, (src, dst) in enumerate(((pg, both_g), (pu, both_u), (pd, both_d))):
        far = pltpu.make_async_remote_copy(
            src_ref=src, dst_ref=dst.at[core], send_sem=p_send.at[i], recv_sem=p_recv.at[i],
            device_id=(me, 1 - core), device_id_type=MESH,
        )
        near = pltpu.make_async_copy(src, dst.at[core], p_loc.at[i])
        far.start()
        near.start()
        ps.append((far, near))

    def sum_copy(ph, t, k):
        q, _, _ = peer_of(me, ORDERS[t][ph], k)
        rows = pl.ds(*SUM_ROWS[t])
        return pltpu.make_async_remote_copy(
            src_ref=sums.at[ph, rows], dst_ref=got.at[ph, k - 1, rows],
            send_sem=r_send.at[ph, t, k - 1], recv_sem=r_recv.at[ph, t, k - 1],
            device_id=(q, core), device_id_type=MESH,
        )

    def send_sums(ph):
        for t in range(3):
            for k in (2, 1, 3):
                sum_copy(ph, t, k).start()

    def take_sums(ph):
        for t in range(3):
            for k in (2, 1, 3):
                sum_copy(ph, t, k).wait_recv()
            rows = pl.ds(*SUM_ROWS[t])
            total = sums[ph, rows, :] + got[ph, 0, rows, :] + got[ph, 1, rows, :] + got[ph, 2, rows, :]
            if ph < 2:
                sums[ph + 1, rows, :] = total
            else:
                scale[rows, :] = mag[rows, :] / jnp.sqrt(total + EPS)

    stages = ((s1g, s1g, s2g, s3g), (su, s1u, s2u, ou), (sd, s1d, s2d, od))

    def far_copy(g, ph, t, k):
        m, thirds = GROUPS[g]
        if m == 0 and ph == 0:
            thirds = G_ROWS
        axis = ORDERS[t][ph]
        p, mine, other = peer_of(me, axis, k)
        return pltpu.make_async_remote_copy(
            src_ref=at(stages[m][ph], axis, other, thirds[t]),
            dst_ref=at(stages[m][ph + 1], axis, mine, thirds[t]),
            send_sem=x_send.at[g, ph, t, k - 1], recv_sem=x_recv.at[g, ph, t, k - 1],
            device_id=(p, core), device_id_type=MESH,
        )

    def near_copy(g, ph, t):
        m, thirds = GROUPS[g]
        if m == 0 and ph == 0:
            thirds = G_ROWS
        axis = ORDERS[t][ph]
        _, mine, _ = peer_of(me, axis, 1)
        return pltpu.make_async_copy(
            at(stages[m][ph], axis, mine, thirds[t]),
            at(stages[m][ph + 1], axis, mine, thirds[t]),
            x_loc.at[g, ph, t],
        )

    def arrive(g, ph, t):
        for k in (2, 1, 3):
            far_copy(g, ph, t, k).wait_recv()
        near_copy(g, ph, t).wait()

    def send(g, ph):
        for t in range(3):
            if ph > 0 and (g, ph) != (1, 1):
                arrive(g, ph - 1, t)
            for k in (2, 1, 3):
                far_copy(g, ph, t, k).start()
            near_copy(g, ph, t).start()

    def send_gate():
        sides = []
        for axis in range(3):
            stride = (16, 4, 1)[axis]
            for k in (2, 1, 3):
                p, mine, other = peer_of(me, axis, k)
                sides.append((axis, k, p, mine, other * stride))
            sides.append((axis, 0, None, mine, mine * stride))

        def go(i, carry):
            for e in range(4):
                for t, rows in enumerate(G_ROWS):
                    for axis, k, p, mine, base in sides:
                        if axis != ORDERS[t][0]:
                            continue
                        ix = [i, e]
                        ix.insert(axis, mine)
                        others = (i * 4 + e, i * 16 + e, i * 16 + e * 4)[axis]
                        start = pl.multiple_of(window(base + others) + rows[0], 8)
                        src = wg.at[pl.ds(start, rows[1])]
                        dst = s1g.at[(*ix, pl.ds(*rows))]
                        if k == 0:
                            pltpu.make_async_copy(src, dst, x_loc.at[0, 0, t]).start()
                        else:
                            pltpu.make_async_remote_copy(
                                src_ref=src, dst_ref=dst,
                                send_sem=x_send.at[0, 0, t, k - 1],
                                recv_sem=x_recv.at[0, 0, t, k - 1],
                                device_id=(p, core), device_id_type=MESH,
                            ).start()
            return carry

        lax.fori_loop(0, 4, go, 0)

    my_half = pl.multiple_of(core * 32, 32)

    def factor_copy(ph, t, k):
        axis = ORDERS[t][ph]
        p, _, _ = peer_of(me, axis, k)
        ix = list(mine_at)
        for done in ORDERS[t][:ph]:
            ix[done] = slice(None)
        first, rows = P_ROWS[t]
        block = gathered.at[(*ix, pl.ds(pl.multiple_of(my_half + first, 16), rows))]
        return pltpu.make_async_remote_copy(
            src_ref=block, dst_ref=block,
            send_sem=g_send.at[ph, t, k - 1], recv_sem=g_recv.at[ph, t, k - 1],
            device_id=(p, core), device_id_type=MESH,
        )

    def send_factor(ph):
        for t in range(2):
            for k in (2, 1, 3):
                factor_copy(ph, t, k).start()

    def take_factor(ph):
        for t in range(2):
            for k in (2, 1, 3):
                factor_copy(ph, t, k).wait_recv()

    def swap_factor():
        block = gathered.at[:, :, :, pl.ds(my_half, 32)]
        return pltpu.make_async_remote_copy(
            src_ref=block, dst_ref=block, send_sem=p_send.at[3], recv_sem=p_recv.at[3],
            device_id=(me, 1 - core), device_id_type=MESH,
        )

    def source(i):
        return lax.div(i, 16), lax.rem(lax.div(i, 4), 4), lax.rem(i, 4)

    start = window(me)
    tile = lax.div(start, 128)
    inner = pl.multiple_of(start - tile * 128, 8)
    skip = me * SLAB - start

    def own_columns():
        @pl.when(me < N - 1)
        def _():
            qwin[...] = rg[:, pl.ds(pl.multiple_of(tile * 128, 128), 384)].astype(F32).T

        @pl.when(me == N - 1)
        def _():
            qwin[0:320, :] = rg[:, COLS - 320 : COLS].astype(F32).T

        qcol[...] = qwin[pl.ds(inner, WIDE), :].astype(BF)
        for e in range(3):
            mcol[e * 128 : (e + 1) * 128, :] = jnp.broadcast_to(
                to_sublanes(mag[pl.ds(tile + e, 1), :], 128), (128, 128)
            )

    def gate_block(i):
        z, y, x = source(i)
        upd = jnp.dot(qcol[...], gathered[z, y, x], preferred_element_type=F32)
        return s3g[z, y, x].astype(F32) + upd

    def gate_squares(i, carry):
        x = gate_block(i)
        acc[...] += x * x
        return carry

    def gate_scale():
        total = jnp.sum(acc[...], axis=1, keepdims=True)
        acc[...] = mcol[pl.ds(inner, WIDE), :] / jnp.sqrt(total + EPS)

    def gate_finish(i, carry):
        shift[0:WIDE, :] = gate_block(i) * acc[...]
        og[:, pl.ds(pl.multiple_of(i * 128, 128), 128)] = shift[pl.ds(skip, SLAB), :].astype(BF)
        return carry

    blocks = COLS // BLK
    tail = blocks * BLK

    def square_blocks(lo, hi, last):
        p = both_u[...].reshape(2 * RANK, RANK)

        def body(b, carry):
            x = combined_t(vu, ru, p, pl.multiple_of(b * BLK, BLK), BLK)
            sums[0, pl.ds(pl.multiple_of(FIRST[1] + b * 8, 8), 8), :] = to_lanes(x * x)
            return carry

        lax.fori_loop(lo, hi, body, 0)
        if last:
            x = combined_t(vu, ru, p, tail, COLS - tail)
            sums[0, FIRST[1] + 112 : FIRST[1] + 116, :] = to_lanes(x * x)
            sums[0, FIRST[1] + 116 : FIRST[1] + 120, :] = jnp.zeros((4, 128), F32)

    def merge_up(h):
        p = both_u[...].reshape(2 * RANK, RANK)
        lo = 7 * h

        def body(b, carry):
            start = pl.multiple_of(b * BLK, BLK)
            x = combined_t(vu, ru, p, start, BLK)
            f = scale[pl.ds(pl.multiple_of(FIRST[1] + b * 8, 8), 8), :]
            for e in range(8):
                to = pl.multiple_of(start - lo * BLK + e * 128, 128)
                full[pl.ds(to, 128), :] = x[e * 128 : (e + 1) * 128] * to_sublanes(f[e : e + 1], 128)
            return carry

        lax.fori_loop(lo, 8 if h == 0 else blocks, body, 0)
        if h == 1:
            x = combined_t(vu, ru, p, tail, COLS - tail)
            f = scale[FIRST[1] + 112 : FIRST[1] + 116, :]
            for e in range(4):
                n = 128 if e < 3 else 64
                to = tail - lo * BLK + e * 128
                full[to : to + n, :] = x[e * 128 : e * 128 + n] * to_sublanes(f[e : e + 1], n)
            end = COLS - lo * BLK
            full[end : end + 8, :] = jnp.zeros((8, 128), F32)

        def cut(g, carry):
            base = pl.multiple_of(g * (8 * SLAB) - lo * BLK, 8)
            for e in range(8):
                su[lax.div(g, 2), lax.rem(g, 2) * 2 + e // 4, e % 4] = full[
                    pl.ds(base + e * SLAB, SLAB + 1), :
                ].astype(BF)
            return carry

        lax.fori_loop(4 * h, 4 * h + 4, cut, 0)

    def down_block(j):
        lanes = pl.ds(pl.multiple_of(j * 128, 128), 128)
        p = pdown[0:DROWS, :].astype(BF)
        upd = jnp.dot(p, rd[:, lanes], preferred_element_type=F32)
        return vd[:, lanes].astype(F32) + upd

    def square_down(j, carry):
        x = down_block(j)
        sums[0, pl.ds(FIRST[2] + j, 1), :] = jnp.sum(x * x, axis=0, keepdims=True)
        return carry

    first = WINDOW - lax.rem(me * DROWS, WINDOW)

    def merge_down(j, carry):
        y = down_block(j) * scale[pl.ds(FIRST[2] + j, 1), :]
        turn[0:DROWS, :] = y
        turn[WINDOW : WINDOW + DROWS, :] = y
        z = turn[pl.ds(first, WINDOW), :].T.astype(BF)
        a, b, c = lax.div(j, 8), lax.rem(lax.div(j, 2), 4), lax.rem(j, 2) * 2
        for e in range(4):
            sd[a, b, c, e * 64 : (e + 1) * 64, :] = z[0:64, e * 128 : (e + 1) * 128]
            sd[a, b, c + 1, e * 64 : (e + 1) * 64, :] = z[64:128, e * 128 : (e + 1) * 128]
        return carry

    send_gate()
    u_loads[1].start()
    q_loads[2].start()
    d_load.start()
    q_loads[0].start()
    for far, near in ps:
        near.wait()
        far.wait()
    turn[...] = jnp.zeros_like(turn)
    acc[...] = jnp.zeros_like(acc)
    qwin[...] = jnp.zeros_like(qwin)
    shift[0:RANK, :] = both_g[...].reshape(2 * RANK, RANK).astype(F32).T
    gathered[(*mine_at, pl.ds(my_half, 32))] = shift[pl.ds(my_half, 32), :].astype(BF)
    q_loads[1].wait()
    u_loads[0].wait()
    square_blocks(0, 7, False)
    send_factor(0)
    u_loads[1].wait()
    square_blocks(7, blocks, True)
    pdown[0:231, :] = both_d[0].astype(F32).T
    pdown[231:462, :] = both_d[1].astype(F32).T
    q_loads[2].wait()
    d_load.wait()
    lax.fori_loop(0, DCOLS // 128, square_down, 0)
    send_sums(0)
    send(0, 1)
    mag[...] = jnp.zeros_like(mag)
    mag[FIRST[2] : FIRST[2] + 32, :] = md[...]
    for top, src in ((FIRST[0], mg), (FIRST[1], mu)):

        def rows(j, carry, top=top, src=src):
            at_lane = pl.multiple_of(j * 128, 128)
            mag[pl.ds(top + j, 1), :] = src[pl.ds(at_lane, 128)].reshape(1, 128)
            return carry

        lax.fori_loop(0, COLS // 128, rows, 0)
        mag[top + 115 : top + 116, 0:64] = src[COLS - 64 : COLS].reshape(1, 64)
    take_sums(0)
    send_sums(1)
    send(1, 1)
    take_factor(0)
    send_factor(1)
    take_sums(1)
    send_sums(2)
    send(0, 2)
    take_sums(2)
    send(1, 2)
    merge_up(0)
    merge_up(1)
    send(2, 0)
    send(3, 0)
    take_factor(1)
    send_factor(2)
    lax.fori_loop(0, DCOLS // 256, merge_down, 0)
    send(2, 1)
    lax.fori_loop(DCOLS // 256, DCOLS // 128, merge_down, 0)
    send(3, 1)
    send(4, 0)
    send(2, 2)
    send(5, 0)
    q_loads[0].wait()
    own_columns()
    take_factor(2)
    swap_factor().start()
    for t in range(3):
        arrive(0, 2, t)
        arrive(1, 2, t)
    send(3, 2)
    swap_factor().wait()
    lax.fori_loop(0, N // 2, gate_squares, 0)
    send(4, 1)
    lax.fori_loop(N // 2, N, gate_squares, 0)
    gate_scale()
    send(5, 1)
    lax.fori_loop(0, N // 2, gate_finish, 0)
    send(4, 2)
    lax.fori_loop(N // 2, N, gate_finish, 0)
    send(5, 2)
    for g in range(2, 6):
        for t in range(3):
            arrive(g, 2, t)
    for g in range(6):
        for ph in range(3):
            if (g, ph) == (1, 0):
                continue
            for t in range(3):
                for k in (1, 2, 3):
                    far_copy(g, ph, t, k).wait_send()
    for ph in range(3):
        for t in range(3):
            for k in (1, 2, 3):
                sum_copy(ph, t, k).wait_send()
                if t < 2:
                    factor_copy(ph, t, k).wait_send()


def merge(wg, wu, wd, qg, qu, qd, pg, pu, pd, mg, mu, md):
    hbm = pl.BlockSpec(memory_space=pl.ANY)
    vmem = pl.BlockSpec(memory_space=pltpu.VMEM)
    wide = (4, 4, 4, WIDE, 128)
    slab = (4, 4, 4, SLAB + 1, 128)
    dslab = (4, 4, 4, 256, 128)
    dma = pltpu.SemaphoreType.DMA
    return pl.pallas_call(
        merge_kernel,
        out_shape=[pltpu.VMEM(s, BF) for s in ((SLAB, N * 128), slab, dslab)]
        + [jax.ShapeDtypeStruct(s, BF) for s in (slab, dslab)],
        in_specs=[hbm] * 6 + [vmem] * 6,
        out_specs=[vmem] * 3 + [hbm] * 2,
        scratch_shapes=[
            pltpu.VMEM((COLS, 128), BF), pltpu.VMEM((DROWS, DCOLS), BF),
            pltpu.VMEM((RANK, COLS), BF), pltpu.VMEM((RANK, COLS), BF),
            pltpu.VMEM((RANK, DCOLS), BF),
            *[pltpu.VMEM(s, BF) for s in (slab, dslab, wide, wide, wide, slab, dslab)],
            pltpu.VMEM((HALF, 128), F32), pltpu.VMEM((2 * WINDOW, 128), F32),
            pltpu.VMEM((2, 64, 64), BF), pltpu.VMEM((2, 64, 64), BF), pltpu.VMEM((2, 64, 231), BF),
            pltpu.VMEM((464, 64), F32), pltpu.VMEM((272, 128), F32),
            pltpu.VMEM((3, 272, 128), F32), pltpu.VMEM((3, 3, 272, 128), F32),
            pltpu.VMEM((272, 128), F32),
            pltpu.VMEM((4, 4, 4, RANK, 128), BF), pltpu.VMEM((384, RANK), F32),
            pltpu.VMEM((WIDE, RANK), BF), pltpu.VMEM((384, 128), F32),
            pltpu.VMEM((WIDE, 128), F32), pltpu.VMEM((WIDE + 8, 128), F32),
            dma((3,)), dma((4,)), dma((4,)), dma((4,)), dma((3,)),
            dma((3, 3, 3)), dma((3, 3, 3)),
            dma((6, 3, 3, 3)), dma((6, 3, 3, 3)), dma((6, 3, 3)),
            dma((3, 2, 3)), dma((3, 2, 3)),
        ],
        compiler_params=pltpu.CompilerParams(
            collective_id=0, has_side_effects=True, vmem_limit_bytes=54 * 10**6
        ),
        name="merge",
    )(wg, wu, wd, qg, qu, qd, pg, pu, pd, mg, mu, md)[:3]


LANES = 1024
TILES = 33
DEPTH = 4


def join_kernel(g, u, d, og, ou, od, bufs, dbufs, gsem, sem, dsem):
    gate = pltpu.make_async_copy(g, og, gsem)
    gate.start()

    def out_down(i):
        lanes = pl.ds(pl.multiple_of(i * (TILES * 128), 128), TILES * 128)
        b = lax.rem(i, DEPTH)
        return pltpu.make_async_copy(dbufs.at[b], od.at[:, lanes], dsem.at[b])

    def step_down(i, carry):
        @pl.when(i >= DEPTH)
        def _():
            out_down(i - DEPTH).wait()

        buf = dbufs.at[lax.rem(i, DEPTH)]

        def tile(j, carry):
            t = i * TILES + j
            s = lax.div(t * 128, DROWS)
            nxt = jnp.minimum(s + 1, N - 1)
            rows = pl.ds(pl.multiple_of(lax.rem(t, 4) * 64, 64), 64)
            lane = t * 128 + lax.broadcasted_iota(jnp.int32, (64, 128), 1)
            buf[:, pl.ds(pl.multiple_of(j * 128, 128), 128)] = jnp.where(
                lane < (s + 1) * DROWS, d[s, rows, :], d[nxt, rows, :]
            )
            return carry

        lax.fori_loop(0, TILES, tile, 0, unroll=11)
        out_down(i).start()
        return carry

    lax.fori_loop(0, 7, step_down, 0)

    def out(i):
        b = lax.rem(i, DEPTH)
        lanes = pl.ds(pl.multiple_of(i * LANES, LANES), LANES)
        return pltpu.make_async_copy(bufs.at[b], ou.at[:, lanes], sem.at[b])

    def step(i, carry):
        @pl.when(i >= DEPTH)
        def _():
            out(i - DEPTH).wait()

        buf = bufs.at[lax.rem(i, DEPTH)]
        for e in range(8):
            buf[:, e * 128 : (e + 1) * 128] = u[i * 8 + e, 0:SLAB, :]
        out(i).start()
        return carry

    lax.fori_loop(0, 8, step, 0)
    for n in range(3, 7):
        out_down(n).wait()
    for n in range(4, 8):
        out(n).wait()
    gate.wait()


def join(g, u, d):
    hbm = pl.BlockSpec(memory_space=pl.ANY)
    vmem = pl.BlockSpec(memory_space=pltpu.VMEM)
    dma = pltpu.SemaphoreType.DMA
    return pl.pallas_call(
        join_kernel,
        out_shape=[jax.ShapeDtypeStruct((SLAB, N * 128), BF)] * 2
        + [jax.ShapeDtypeStruct((64, N * DROWS), BF)],
        in_specs=[vmem] * 3,
        out_specs=[hbm] * 3,
        scratch_shapes=[
            pltpu.VMEM((DEPTH, SLAB, LANES), BF), pltpu.VMEM((DEPTH, 64, TILES * 128), BF),
            dma, dma((DEPTH,)), dma((DEPTH,)),
        ],
        compiler_params=pltpu.CompilerParams(vmem_limit_bytes=16 * 2**20),
        name="join",
    )(g, u.reshape(N, SLAB + 1, 128), d.reshape(N, 256, 128))


def local(wg, wu, wd, pg, qg, pu, qu, pd, qd, mg, mu, md):
    g, u, d = merge(wg.T, wu.T, wd, qg, qu, qd, pg, pu, pd.T, mg, mu, md.reshape(32, 128))
    return tuple(o.T for o in join(g, u, d))


def solution(mesh):
    placed = (
        P("row", "col"),
        P("row", "col"),
        P("row", "col"),
        P(("row", "col"), None),
        P(None, "col"),
        P(("row", "col"), None),
        P(None, "col"),
        P(("row", "col"), None),
        P(None, "col"),
        P("col"),
        P("col"),
        P("col"),
    )
    return jax.shard_map(
        local,
        mesh=mesh,
        in_specs=placed,
        out_specs=(P(None, ("col", "row")), P(None, ("col", "row")), P(None, ("col", "row"))),
        check_vma=False,
    )
```

```python
import functools

import jax
import jax.numpy as jnp
from jax import lax
from jax.experimental import pallas as pl
from jax.experimental.pallas import tpu as pltpu
from jax.sharding import PartitionSpec as P

MESH = pl.DeviceIdType.MESH
BF = jnp.bfloat16
F32 = jnp.float32
EPS = 1e-06
RANK = 64
N = 64
COLS = 14784
SLAB = 231
DROWS = 462
DCOLS = 4096
WINDOW = 512
WIDE = 240
BLK = 1024
HALF = 8 * BLK
ORDERS = ((2, 1, 0), (1, 0, 2), (0, 2, 1))
FIRST = (0, 120, 240)
SUM_ROWS = ((120, 48), (168, 56), (224, 48))
GROUPS = (
    (0, ((0, 48), (80, 48), (160, 48))),
    (0, ((48, 32), (128, 32), (208, 32))),
    (1, ((0, 48), (80, 48), (160, 48))),
    (1, ((48, 32), (128, 32), (208, 24))),
    (2, ((0, 48), (80, 48), (176, 48))),
    (2, ((48, 32), (128, 48), (224, 32))),
)
G_ROWS = ((0, 80), (80, 80), (160, 80))
P_ROWS = ((0, 16), (16, 16))


def peer_of(me, axis, k):
    stride = (16, 4, 1)[axis]
    mine = lax.rem(lax.div(me, stride), 4)
    other = lax.rem(mine + k, 4)
    return me + (other - mine) * stride, mine, other


def greet(me, core):
    bar = pltpu.get_barrier_semaphore()
    for axis in range(3):
        for k in (1, 2, 3):
            p, _, _ = peer_of(me, axis, k)
            pl.semaphore_signal(bar, inc=1, device_id=(p, core), device_id_type=MESH)
    pl.semaphore_signal(bar, inc=1, device_id=(me, 1 - core), device_id_type=MESH)
    pl.semaphore_wait(bar, 10)


def eye(h):
    return lax.broadcasted_iota(jnp.int32, (h, 128), 0) == lax.broadcasted_iota(
        jnp.int32, (h, 128), 1
    )


def to_lanes(x):
    n = x.shape[0]
    sums = jnp.sum(x, axis=1, keepdims=True)
    rows = []
    for b in range(0, n, 128):
        h = min(128, n - b)
        rows.append(jnp.sum(jnp.where(eye(h), sums[b : b + h], 0.0), axis=0, keepdims=True))
    return jnp.concatenate(rows, axis=0)


def to_sublanes(row, h):
    return jnp.sum(jnp.where(eye(h), row, 0.0), axis=1, keepdims=True)


def combined_t(w, q, p, start, n):
    upd = lax.dot_general(
        q[:, pl.ds(start, n)], p, (((0,), (1,)), ((), ())), preferred_element_type=F32
    )
    return w[pl.ds(start, n), :].astype(F32) + upd


def at(ref, axis, idx, rows):
    ix = [slice(None)] * 3
    ix[axis] = idx
    return ref.at[(*ix, pl.ds(*rows))]


def window(s):
    return jnp.minimum(lax.div(s * SLAB, 8) * 8, COLS - WIDE)


def merge_kernel(
    wg, wu, wd, qg, qu, qd, pg, pu, pd, mg, mu, md,
    og, ou, od, s1u, s1d,
    vu, vd, rg, ru, rd, su, sd, s1g, s2g, s3g, s2u, s2d,
    full, turn, both_g, both_u, both_d, pdown, mag, sums, got, scale,
    gathered, qwin, qcol, mcol, acc, shift,
    w_sem, q_sem, p_send, p_recv, p_loc, r_send, r_recv, x_send, x_recv, x_loc,
    g_send, g_recv,
):
    me = lax.axis_index("row")
    core = lax.axis_index("col")
    mine_at = (lax.div(me, 16), lax.rem(lax.div(me, 4), 4), lax.rem(me, 4))
    half = 7 * BLK
    u_loads = [
        pltpu.make_async_copy(wu.at[part], vu.at[part], w_sem.at[h])
        for h, part in enumerate((pl.ds(0, half), pl.ds(half, COLS - half)))
    ]
    d_load = pltpu.make_async_copy(wd, vd, w_sem.at[2])
    q_loads = [
        pltpu.make_async_copy(src, dst, q_sem.at[i])
        for i, (src, dst) in enumerate(((qg, rg), (qu, ru), (qd, rd)))
    ]
    q_loads[1].start()
    u_loads[0].start()
    greet(me, core)
    ps = []
    for i, (src, dst) in enumerate(((pg, both_g), (pu, both_u), (pd, both_d))):
        far = pltpu.make_async_remote_copy(
            src_ref=src, dst_ref=dst.at[core], send_sem=p_send.at[i], recv_sem=p_recv.at[i],
            device_id=(me, 1 - core), device_id_type=MESH,
        )
        near = pltpu.make_async_copy(src, dst.at[core], p_loc.at[i])
        far.start()
        near.start()
        ps.append((far, near))

    def sum_copy(ph, t, k):
        q, _, _ = peer_of(me, ORDERS[t][ph], k)
        rows = pl.ds(*SUM_ROWS[t])
        return pltpu.make_async_remote_copy(
            src_ref=sums.at[ph, rows], dst_ref=got.at[ph, k - 1, rows],
            send_sem=r_send.at[ph, t, k - 1], recv_sem=r_recv.at[ph, t, k - 1],
            device_id=(q, core), device_id_type=MESH,
        )

    def send_sums(ph):
        for t in range(3):
            for k in (2, 1, 3):
                sum_copy(ph, t, k).start()

    def take_sums(ph):
        for t in range(3):
            for k in (2, 1, 3):
                sum_copy(ph, t, k).wait_recv()
            rows = pl.ds(*SUM_ROWS[t])
            total = sums[ph, rows, :] + got[ph, 0, rows, :] + got[ph, 1, rows, :] + got[ph, 2, rows, :]
            if ph < 2:
                sums[ph + 1, rows, :] = total
            else:
                scale[rows, :] = mag[rows, :] / jnp.sqrt(total + EPS)

    stages = ((s1g, s1g, s2g, s3g), (su, s1u, s2u, ou), (sd, s1d, s2d, od))

    def far_copy(g, ph, t, k):
        m, thirds = GROUPS[g]
        if m == 0 and ph == 0:
            thirds = G_ROWS
        axis = ORDERS[t][ph]
        p, mine, other = peer_of(me, axis, k)
        return pltpu.make_async_remote_copy(
            src_ref=at(stages[m][ph], axis, other, thirds[t]),
            dst_ref=at(stages[m][ph + 1], axis, mine, thirds[t]),
            send_sem=x_send.at[g, ph, t, k - 1], recv_sem=x_recv.at[g, ph, t, k - 1],
            device_id=(p, core), device_id_type=MESH,
        )

    def near_copy(g, ph, t):
        m, thirds = GROUPS[g]
        if m == 0 and ph == 0:
            thirds = G_ROWS
        axis = ORDERS[t][ph]
        _, mine, _ = peer_of(me, axis, 1)
        return pltpu.make_async_copy(
            at(stages[m][ph], axis, mine, thirds[t]),
            at(stages[m][ph + 1], axis, mine, thirds[t]),
            x_loc.at[g, ph, t],
        )

    def arrive(g, ph, t):
        for k in (2, 1, 3):
            far_copy(g, ph, t, k).wait_recv()
        near_copy(g, ph, t).wait()

    def send(g, ph):
        for t in range(3):
            if ph > 0 and (g, ph) != (1, 1):
                arrive(g, ph - 1, t)
            for k in (2, 1, 3):
                far_copy(g, ph, t, k).start()
            near_copy(g, ph, t).start()

    def send_gate():
        sides = []
        for axis in range(3):
            stride = (16, 4, 1)[axis]
            for k in (2, 1, 3):
                p, mine, other = peer_of(me, axis, k)
                sides.append((axis, k, p, mine, other * stride))
            sides.append((axis, 0, None, mine, mine * stride))

        def go(i, carry):
            for e in range(4):
                for t, rows in enumerate(G_ROWS):
                    for axis, k, p, mine, base in sides:
                        if axis != ORDERS[t][0]:
                            continue
                        ix = [i, e]
                        ix.insert(axis, mine)
                        others = (i * 4 + e, i * 16 + e, i * 16 + e * 4)[axis]
                        start = pl.multiple_of(window(base + others) + rows[0], 8)
                        src = wg.at[pl.ds(start, rows[1])]
                        dst = s1g.at[(*ix, pl.ds(*rows))]
                        if k == 0:
                            pltpu.make_async_copy(src, dst, x_loc.at[0, 0, t]).start()
                        else:
                            pltpu.make_async_remote_copy(
                                src_ref=src, dst_ref=dst,
                                send_sem=x_send.at[0, 0, t, k - 1],
                                recv_sem=x_recv.at[0, 0, t, k - 1],
                                device_id=(p, core), device_id_type=MESH,
                            ).start()
            return carry

        lax.fori_loop(0, 4, go, 0)

    my_half = pl.multiple_of(core * 32, 32)

    def factor_copy(ph, t, k):
        axis = ORDERS[t][ph]
        p, _, _ = peer_of(me, axis, k)
        ix = list(mine_at)
        for done in ORDERS[t][:ph]:
            ix[done] = slice(None)
        first, rows = P_ROWS[t]
        block = gathered.at[(*ix, pl.ds(pl.multiple_of(my_half + first, 16), rows))]
        return pltpu.make_async_remote_copy(
            src_ref=block, dst_ref=block,
            send_sem=g_send.at[ph, t, k - 1], recv_sem=g_recv.at[ph, t, k - 1],
            device_id=(p, core), device_id_type=MESH,
        )

    def send_factor(ph):
        for t in range(2):
            for k in (2, 1, 3):
                factor_copy(ph, t, k).start()

    def take_factor(ph):
        for t in range(2):
            for k in (2, 1, 3):
                factor_copy(ph, t, k).wait_recv()

    def swap_factor():
        block = gathered.at[:, :, :, pl.ds(my_half, 32)]
        return pltpu.make_async_remote_copy(
            src_ref=block, dst_ref=block, send_sem=p_send.at[3], recv_sem=p_recv.at[3],
            device_id=(me, 1 - core), device_id_type=MESH,
        )

    def source(i):
        return lax.div(i, 16), lax.rem(lax.div(i, 4), 4), lax.rem(i, 4)

    start = window(me)
    tile = lax.div(start, 128)
    inner = pl.multiple_of(start - tile * 128, 8)
    skip = me * SLAB - start

    def own_columns():
        @pl.when(me < N - 1)
        def _():
            qwin[...] = rg[:, pl.ds(pl.multiple_of(tile * 128, 128), 384)].astype(F32).T

        @pl.when(me == N - 1)
        def _():
            qwin[0:320, :] = rg[:, COLS - 320 : COLS].astype(F32).T

        qcol[...] = qwin[pl.ds(inner, WIDE), :].astype(BF)
        for e in range(3):
            mcol[e * 128 : (e + 1) * 128, :] = jnp.broadcast_to(
                to_sublanes(mag[pl.ds(tile + e, 1), :], 128), (128, 128)
            )

    def gate_block(i):
        z, y, x = source(i)
        upd = jnp.dot(qcol[...], gathered[z, y, x], preferred_element_type=F32)
        return s3g[z, y, x].astype(F32) + upd

    def gate_squares(i, carry):
        x = gate_block(i)
        acc[...] += x * x
        return carry

    def gate_scale():
        total = jnp.sum(acc[...], axis=1, keepdims=True)
        acc[...] = mcol[pl.ds(inner, WIDE), :] / jnp.sqrt(total + EPS)

    def gate_finish(i, carry):
        shift[0:WIDE, :] = gate_block(i) * acc[...]
        og[:, pl.ds(pl.multiple_of(i * 128, 128), 128)] = shift[pl.ds(skip, SLAB), :].astype(BF)
        return carry

    blocks = COLS // BLK
    tail = blocks * BLK

    def square_blocks(lo, hi, last):
        p = both_u[...].reshape(2 * RANK, RANK)

        def body(b, carry):
            x = combined_t(vu, ru, p, pl.multiple_of(b * BLK, BLK), BLK)
            sums[0, pl.ds(pl.multiple_of(FIRST[1] + b * 8, 8), 8), :] = to_lanes(x * x)
            return carry

        lax.fori_loop(lo, hi, body, 0)
        if last:
            x = combined_t(vu, ru, p, tail, COLS - tail)
            sums[0, FIRST[1] + 112 : FIRST[1] + 116, :] = to_lanes(x * x)
            sums[0, FIRST[1] + 116 : FIRST[1] + 120, :] = jnp.zeros((4, 128), F32)

    def merge_up(h):
        p = both_u[...].reshape(2 * RANK, RANK)
        lo = 7 * h

        def body(b, carry):
            start = pl.multiple_of(b * BLK, BLK)
            x = combined_t(vu, ru, p, start, BLK)
            f = scale[pl.ds(pl.multiple_of(FIRST[1] + b * 8, 8), 8), :]
            for e in range(8):
                to = pl.multiple_of(start - lo * BLK + e * 128, 128)
                full[pl.ds(to, 128), :] = x[e * 128 : (e + 1) * 128] * to_sublanes(f[e : e + 1], 128)
            return carry

        lax.fori_loop(lo, 8 if h == 0 else blocks, body, 0)
        if h == 1:
            x = combined_t(vu, ru, p, tail, COLS - tail)
            f = scale[FIRST[1] + 112 : FIRST[1] + 116, :]
            for e in range(4):
                n = 128 if e < 3 else 64
                to = tail - lo * BLK + e * 128
                full[to : to + n, :] = x[e * 128 : e * 128 + n] * to_sublanes(f[e : e + 1], n)
            end = COLS - lo * BLK
            full[end : end + 8, :] = jnp.zeros((8, 128), F32)

        def cut(g, carry):
            base = pl.multiple_of(g * (8 * SLAB) - lo * BLK, 8)
            for e in range(8):
                su[lax.div(g, 2), lax.rem(g, 2) * 2 + e // 4, e % 4] = full[
                    pl.ds(base + e * SLAB, SLAB + 1), :
                ].astype(BF)
            return carry

        lax.fori_loop(4 * h, 4 * h + 4, cut, 0)

    def down_block(j):
        lanes = pl.ds(pl.multiple_of(j * 128, 128), 128)
        p = pdown[0:DROWS, :].astype(BF)
        upd = jnp.dot(p, rd[:, lanes], preferred_element_type=F32)
        return vd[:, lanes].astype(F32) + upd

    def square_down(j, carry):
        x = down_block(j)
        sums[0, pl.ds(FIRST[2] + j, 1), :] = jnp.sum(x * x, axis=0, keepdims=True)
        return carry

    first = WINDOW - lax.rem(me * DROWS, WINDOW)

    def merge_down(j, carry):
        y = down_block(j) * scale[pl.ds(FIRST[2] + j, 1), :]
        turn[0:DROWS, :] = y
        turn[WINDOW : WINDOW + DROWS, :] = y
        z = turn[pl.ds(first, WINDOW), :].T.astype(BF)
        a, b, c = lax.div(j, 8), lax.rem(lax.div(j, 2), 4), lax.rem(j, 2) * 2
        for e in range(4):
            sd[a, b, c, e * 64 : (e + 1) * 64, :] = z[0:64, e * 128 : (e + 1) * 128]
            sd[a, b, c + 1, e * 64 : (e + 1) * 64, :] = z[64:128, e * 128 : (e + 1) * 128]
        return carry

    send_gate()
    u_loads[1].start()
    q_loads[2].start()
    d_load.start()
    q_loads[0].start()
    for far, near in ps:
        near.wait()
        far.wait()
    turn[...] = jnp.zeros_like(turn)
    acc[...] = jnp.zeros_like(acc)
    qwin[...] = jnp.zeros_like(qwin)
    shift[0:RANK, :] = both_g[...].reshape(2 * RANK, RANK).astype(F32).T
    gathered[(*mine_at, pl.ds(my_half, 32))] = shift[pl.ds(my_half, 32), :].astype(BF)
    q_loads[1].wait()
    u_loads[0].wait()
    square_blocks(0, 7, False)
    send_factor(0)
    u_loads[1].wait()
    square_blocks(7, blocks, True)
    pdown[0:231, :] = both_d[0].astype(F32).T
    pdown[231:462, :] = both_d[1].astype(F32).T
    q_loads[2].wait()
    d_load.wait()
    lax.fori_loop(0, DCOLS // 128, square_down, 0)
    send_sums(0)
    send(0, 1)
    mag[...] = jnp.zeros_like(mag)
    mag[FIRST[2] : FIRST[2] + 32, :] = md[...]
    for top, src in ((FIRST[0], mg), (FIRST[1], mu)):

        def rows(j, carry, top=top, src=src):
            at_lane = pl.multiple_of(j * 128, 128)
            mag[pl.ds(top + j, 1), :] = src[pl.ds(at_lane, 128)].reshape(1, 128)
            return carry

        lax.fori_loop(0, COLS // 128, rows, 0)
        mag[top + 115 : top + 116, 0:64] = src[COLS - 64 : COLS].reshape(1, 64)
    take_sums(0)
    send_sums(1)
    send(1, 1)
    take_factor(0)
    send_factor(1)
    take_sums(1)
    send_sums(2)
    send(0, 2)
    take_sums(2)
    send(1, 2)
    merge_up(0)
    merge_up(1)
    send(2, 0)
    send(3, 0)
    take_factor(1)
    send_factor(2)
    lax.fori_loop(0, DCOLS // 256, merge_down, 0)
    send(2, 1)
    lax.fori_loop(DCOLS // 256, DCOLS // 128, merge_down, 0)
    send(3, 1)
    send(4, 0)
    send(2, 2)
    send(5, 0)
    send(3, 2)
    q_loads[0].wait()
    own_columns()
    take_factor(2)
    swap_factor().start()
    for t in range(3):
        arrive(0, 2, t)
        arrive(1, 2, t)
    swap_factor().wait()
    lax.fori_loop(0, N // 2, gate_squares, 0)
    send(4, 1)
    lax.fori_loop(N // 2, N, gate_squares, 0)
    gate_scale()
    send(5, 1)
    lax.fori_loop(0, N // 2, gate_finish, 0)
    send(4, 2)
    lax.fori_loop(N // 2, N, gate_finish, 0)
    send(5, 2)
    for g in range(2, 6):
        for t in range(3):
            arrive(g, 2, t)
    for g in range(6):
        for ph in range(3):
            if (g, ph) == (1, 0):
                continue
            for t in range(3):
                for k in (1, 2, 3):
                    far_copy(g, ph, t, k).wait_send()
    for ph in range(3):
        for t in range(3):
            for k in (1, 2, 3):
                sum_copy(ph, t, k).wait_send()
                if t < 2:
                    factor_copy(ph, t, k).wait_send()


def merge(wg, wu, wd, qg, qu, qd, pg, pu, pd, mg, mu, md):
    hbm = pl.BlockSpec(memory_space=pl.ANY)
    vmem = pl.BlockSpec(memory_space=pltpu.VMEM)
    wide = (4, 4, 4, WIDE, 128)
    slab = (4, 4, 4, SLAB + 1, 128)
    dslab = (4, 4, 4, 256, 128)
    dma = pltpu.SemaphoreType.DMA
    return pl.pallas_call(
        merge_kernel,
        out_shape=[pltpu.VMEM(s, BF) for s in ((SLAB, N * 128), slab, dslab)]
        + [jax.ShapeDtypeStruct(s, BF) for s in (slab, dslab)],
        in_specs=[hbm] * 6 + [vmem] * 6,
        out_specs=[vmem] * 3 + [hbm] * 2,
        scratch_shapes=[
            pltpu.VMEM((COLS, 128), BF), pltpu.VMEM((DROWS, DCOLS), BF),
            pltpu.VMEM((RANK, COLS), BF), pltpu.VMEM((RANK, COLS), BF),
            pltpu.VMEM((RANK, DCOLS), BF),
            *[pltpu.VMEM(s, BF) for s in (slab, dslab, wide, wide, wide, slab, dslab)],
            pltpu.VMEM((HALF, 128), F32), pltpu.VMEM((2 * WINDOW, 128), F32),
            pltpu.VMEM((2, 64, 64), BF), pltpu.VMEM((2, 64, 64), BF), pltpu.VMEM((2, 64, 231), BF),
            pltpu.VMEM((464, 64), F32), pltpu.VMEM((272, 128), F32),
            pltpu.VMEM((3, 272, 128), F32), pltpu.VMEM((3, 3, 272, 128), F32),
            pltpu.VMEM((272, 128), F32),
            pltpu.VMEM((4, 4, 4, RANK, 128), BF), pltpu.VMEM((384, RANK), F32),
            pltpu.VMEM((WIDE, RANK), BF), pltpu.VMEM((384, 128), F32),
            pltpu.VMEM((WIDE, 128), F32), pltpu.VMEM((WIDE + 8, 128), F32),
            dma((3,)), dma((4,)), dma((4,)), dma((4,)), dma((3,)),
            dma((3, 3, 3)), dma((3, 3, 3)),
            dma((6, 3, 3, 3)), dma((6, 3, 3, 3)), dma((6, 3, 3)),
            dma((3, 2, 3)), dma((3, 2, 3)),
        ],
        compiler_params=pltpu.CompilerParams(
            collective_id=0, has_side_effects=True, vmem_limit_bytes=54 * 10**6
        ),
        name="merge",
    )(wg, wu, wd, qg, qu, qd, pg, pu, pd, mg, mu, md)[:3]


LANES = 1024
TILES = 33
DEPTH = 4


def join_kernel(g, u, d, og, ou, od, bufs, dbufs, gsem, sem, dsem):
    gate = pltpu.make_async_copy(g, og, gsem)
    gate.start()

    def out_down(i):
        lanes = pl.ds(pl.multiple_of(i * (TILES * 128), 128), TILES * 128)
        b = lax.rem(i, DEPTH)
        return pltpu.make_async_copy(dbufs.at[b], od.at[:, lanes], dsem.at[b])

    def step_down(i, carry):
        @pl.when(i >= DEPTH)
        def _():
            out_down(i - DEPTH).wait()

        buf = dbufs.at[lax.rem(i, DEPTH)]

        def tile(j, carry):
            t = i * TILES + j
            s = lax.div(t * 128, DROWS)
            nxt = jnp.minimum(s + 1, N - 1)
            rows = pl.ds(pl.multiple_of(lax.rem(t, 4) * 64, 64), 64)
            lane = t * 128 + lax.broadcasted_iota(jnp.int32, (64, 128), 1)
            buf[:, pl.ds(pl.multiple_of(j * 128, 128), 128)] = jnp.where(
                lane < (s + 1) * DROWS, d[s, rows, :], d[nxt, rows, :]
            )
            return carry

        lax.fori_loop(0, TILES, tile, 0, unroll=11)
        out_down(i).start()
        return carry

    lax.fori_loop(0, 7, step_down, 0)

    def out(i):
        b = lax.rem(i, DEPTH)
        lanes = pl.ds(pl.multiple_of(i * LANES, LANES), LANES)
        return pltpu.make_async_copy(bufs.at[b], ou.at[:, lanes], sem.at[b])

    def step(i, carry):
        @pl.when(i >= DEPTH)
        def _():
            out(i - DEPTH).wait()

        buf = bufs.at[lax.rem(i, DEPTH)]
        for e in range(8):
            buf[:, e * 128 : (e + 1) * 128] = u[i * 8 + e, 0:SLAB, :]
        out(i).start()
        return carry

    lax.fori_loop(0, 8, step, 0)
    for n in range(3, 7):
        out_down(n).wait()
    for n in range(4, 8):
        out(n).wait()
    gate.wait()


def join(g, u, d):
    hbm = pl.BlockSpec(memory_space=pl.ANY)
    vmem = pl.BlockSpec(memory_space=pltpu.VMEM)
    dma = pltpu.SemaphoreType.DMA
    return pl.pallas_call(
        join_kernel,
        out_shape=[jax.ShapeDtypeStruct((SLAB, N * 128), BF)] * 2
        + [jax.ShapeDtypeStruct((64, N * DROWS), BF)],
        in_specs=[vmem] * 3,
        out_specs=[hbm] * 3,
        scratch_shapes=[
            pltpu.VMEM((DEPTH, SLAB, LANES), BF), pltpu.VMEM((DEPTH, 64, TILES * 128), BF),
            dma, dma((DEPTH,)), dma((DEPTH,)),
        ],
        compiler_params=pltpu.CompilerParams(vmem_limit_bytes=16 * 2**20),
        name="join",
    )(g, u.reshape(N, SLAB + 1, 128), d.reshape(N, 256, 128))


def local(wg, wu, wd, pg, qg, pu, qu, pd, qd, mg, mu, md):
    g, u, d = merge(wg.T, wu.T, wd, qg, qu, qd, pg, pu, pd.T, mg, mu, md.reshape(32, 128))
    return tuple(o.T for o in join(g, u, d))


def solution(mesh):
    placed = (
        P("row", "col"),
        P("row", "col"),
        P("row", "col"),
        P(("row", "col"), None),
        P(None, "col"),
        P(("row", "col"), None),
        P(None, "col"),
        P(("row", "col"), None),
        P(None, "col"),
        P("col"),
        P("col"),
        P("col"),
    )
    return jax.shard_map(
        local,
        mesh=mesh,
        in_specs=placed,
        out_specs=(P(None, ("col", "row")), P(None, ("col", "row")), P(None, ("col", "row"))),
        check_vma=False,
    )
```
